32 devices in a mesh: groups: 2 (over y), feat: 8 (over z, x), rows: 2 (over core).
Axes of the slice: x: 2, y: 2, z: 4, core: 2. Of those that a mesh axis runs over, the one named last changes fastest.
Arguments:
- embeddings: bfloat16 [4096, 8192], P('feat', ('groups', 'rows')), parts along dimension 1, may hold values from -240 to 240
- signs: int32 [4096], P('feat'), may hold values from -1 to 1, as said below
- tile_blocks: int32 [4, 8, 3], P('groups', 'feat'), parts along dimension 0, may hold values from 0 to 15, as said below
- tile_counts: int32 [4, 8], P('groups', 'feat'), parts along dimension 0, may hold values from 1 to 3, as said below
Outputs:
- scores: float32 [4, 8, 3, 256, 256], P(('groups', 'rows'), 'feat'), parts along dimension 0
- unit_rows: bfloat16 [4, 2048, 4096], P(('groups', 'rows'), 'feat'), parts along dimension 0
The draws below stay inside these ranges and needn't reach their ends.
There are 2 independent parts, one for each index of `groups`. The reference program is written for one: setup_inputs(seed, part) draws one part's arguments, and reference() takes and returns one part's arrays. A program takes and returns all parts, laid end to end along the dimension named above; an argument that names none is the same for every part. Nothing has to cross between parts.
Inputs may be any that keep to these rules, and one draw needn't show every extreme that they name: `signs`: every entry is -1 or 1. `tile_blocks`: the 3 entries of owner (r, f) are distinct ids taken from f, 8 + f, (f + 1) % 8 and 8 + (f + 1) % 8; entries at or beyond the owner's count also hold such ids. `tile_counts`: some owner lists 3 tiles in every draw.
All inputs are finite; a program needn't handle non-finite values.
Results may differ from the reference program's by a relative error of at most 0.0015.
Values may be sent and summed in bfloat16 or wider, within the bound.
No kernel may reach another device: no remote copies, remote signals or barrier semaphores. Data moves between devices by JAX's collectives and lax.ppermute only.
A program may use at most 64 MiB of HBM per device.

```python
import math
import jax
import jax.numpy as jnp
from jax import lax

D = 4096
BLOCK = 256
TILES = 3
BUCKETS = 8
HALVES = 2
ROWS = 4096


def draw_embeddings(key, part):
    normal_key, row_key, column_key = jax.random.split(key, 3)
    base_values = jnp.clip(jax.random.normal(normal_key, (ROWS, D), jnp.float32), -5.0, 5.0)
    row_scale = jnp.exp(jax.random.uniform(row_key, (ROWS, 1), jnp.float32, 0.0, math.log(10.0)))
    column_scale = jnp.exp(jax.random.uniform(column_key, (1, D), jnp.float32, 0.0, math.log(3.0)))
    return (base_values * row_scale * column_scale).T.astype(jnp.bfloat16)


def draw_signs(key, part):
    coins = jax.random.randint(key, (D,), 0, 2, dtype=jnp.int32)
    return 2 * coins - 1


def draw_tile_blocks(key, part):
    order_key = jax.random.fold_in(key, 11)
    ranking = jax.random.randint(order_key, (HALVES, BUCKETS, 4), 0, 1 << 20, dtype=jnp.int32) * 4 + jnp.arange(4, dtype=jnp.int32)
    ordering = jnp.argsort(ranking, axis=2, stable=True)
    buckets_here = jnp.arange(BUCKETS, dtype=jnp.int32)[None, :, None]
    buckets_next = (buckets_here + 1) % BUCKETS
    pool_ids = jnp.concatenate([buckets_here, BUCKETS + buckets_here, buckets_next, BUCKETS + buckets_next], axis=2)
    pool_ids = jnp.broadcast_to(pool_ids, (HALVES, BUCKETS, 4))
    chosen = jnp.take_along_axis(pool_ids, ordering, axis=2)
    return chosen[:, :, :TILES].astype(jnp.int32)


def draw_tile_counts(key, part):
    count_key = jax.random.fold_in(key, 23)
    heavy_key, which_key, forced_key = jax.random.split(count_key, 3)
    heavy_pairs = jax.random.randint(heavy_key, (BUCKETS,), 0, 2, dtype=jnp.int32)
    heavy_member = jax.random.randint(which_key, (BUCKETS,), 0, 2, dtype=jnp.int32)
    forced_pair = jax.random.randint(forced_key, (), 0, BUCKETS, dtype=jnp.int32)
    heavy_pairs = jnp.where(jnp.arange(BUCKETS, dtype=jnp.int32) == forced_pair, 1, heavy_pairs)
    half_index = jnp.arange(HALVES, dtype=jnp.int32)[:, None]
    loaded = heavy_pairs[None, :] * (half_index == heavy_member[None, :]).astype(jnp.int32)
    return (1 + (TILES - 1) * loaded).astype(jnp.int32)


def setup_inputs(seed: int = 0, part: int = 0) -> dict:
    streams_of = jax.random.split(jax.random.key(seed), 5)
    part_keys = jax.random.split(jax.random.fold_in(streams_of[4], part), 5)
    embeddings = draw_embeddings(jax.random.fold_in(jax.random.fold_in(streams_of[4], part), 71), part)
    signs = draw_signs(jax.random.fold_in(streams_of[4], 71), part)
    tile_blocks = draw_tile_blocks(jax.random.fold_in(jax.random.fold_in(streams_of[4], part), 71), part)
    tile_counts = draw_tile_counts(jax.random.fold_in(jax.random.fold_in(streams_of[4], part), 71), part)
    return {"embeddings": embeddings, "signs": signs, "tile_blocks": tile_blocks, "tile_counts": tile_counts}


def hadamard(length, number_type):
    positions = jnp.arange(length, dtype=jnp.int32)
    intersection = positions[:, None] & positions[None, :]
    parity = jnp.zeros((length, length), jnp.int32)
    for level in range(max(length.bit_length() - 1, 0)):
        parity = parity + (intersection >> level & 1)
    return (1 - 2 * (parity & 1)).astype(number_type)

def reference(embeddings, signs, tile_blocks, tile_counts):
    upper_width = 2 ** ((D.bit_length() - 1) // 2)
    lower_width = D // upper_width
    inner_table = hadamard(lower_width, jnp.float32)
    outer_table = hadamard(upper_width, jnp.float32)
    score_scale = 1.0 / math.sqrt(D)
    signed = (embeddings * signs.astype(jnp.bfloat16)[:, None]).T
    blocked = signed.reshape(HALVES * BUCKETS, BLOCK, upper_width, lower_width)

    def rotate(piece):
        first_section = jnp.einsum('rab,bc->rac', piece.astype(jnp.float32), inner_table, precision=lax.Precision.HIGHEST)
        turned = jnp.einsum('rac,ad->rdc', first_section, outer_table, precision=lax.Precision.HIGHEST) * score_scale
        flattened = turned.reshape(BLOCK, D)
        norm_factor = lax.rsqrt(lax.optimization_barrier(jnp.mean(flattened * flattened, axis=1, keepdims=True)) + 1e-06)
        return (flattened * norm_factor).astype(jnp.bfloat16)
    unit_blocks = lax.map(rotate, blocked)
    owner_ids = jnp.arange(HALVES * BUCKETS, dtype=jnp.int32)
    flat_lists = tile_blocks.reshape(HALVES * BUCKETS, TILES)
    flat_counts = tile_counts.reshape(HALVES * BUCKETS)

    def score_owner(packed):
        owner_id, owner_list, owner_count = packed
        queries = unit_blocks[owner_id]

        def add_tile(slot_index, buffer):
            keyed_block = unit_blocks[owner_list[slot_index]]
            tile_value = jnp.dot(queries, keyed_block.T, preferred_element_type=jnp.float32) * score_scale
            return lax.dynamic_update_index_in_dim(buffer, tile_value, slot_index, 0)
        return lax.fori_loop(0, owner_count, add_tile, jnp.zeros((TILES, BLOCK, BLOCK), jnp.float32))
    scores = lax.map(score_owner, (owner_ids, flat_lists, flat_counts))
    unit_rows = unit_blocks.reshape(HALVES, BUCKETS * BLOCK, D)
    return (scores.reshape(HALVES, BUCKETS, TILES, BLOCK, BLOCK), unit_rows)
```

```python
import functools
import math

import jax
import jax.numpy as jnp
import numpy as np
from jax import lax
from jax.experimental import pallas as pl
from jax.experimental.pallas import tpu as pltpu
from jax.sharding import PartitionSpec as P

ANY = pl.BlockSpec(memory_space=pl.ANY)
SMEM = pl.BlockSpec(memory_space=pltpu.SMEM)
VMEM_LIMIT = 40 << 20


def parity_table(length):
    positions = np.arange(length)
    shared = positions[:, None] & positions[None, :]
    parity = np.zeros_like(shared)
    while shared.any():
        parity ^= shared & 1
        shared = shared >> 1
    return 1 - 2 * parity


def from_partner(block, axis, distance):
    count = lax.axis_size(axis)
    route = []
    for low in range(count):
        high = low | 1 << distance
        if high != low and high < count:
            route += [(low, high), (high, low)]
    return lax.ppermute(block, axis, route)


def passed_along(value, axis, steps):
    count = lax.axis_size(axis)
    pairs = [(source, (source + steps) % count) for source in range(count)]
    return lax.ppermute(value, axis, pairs)


def general(embeddings, signs, tile_blocks, tile_counts):
    groups = lax.axis_size("feat")
    feat_place = lax.axis_index("feat")
    row_place = lax.axis_index("rows")
    signed = embeddings * signs.astype(jnp.bfloat16)[:, None]
    regrouped = lax.all_to_all(signed, "feat", split_axis=1, concat_axis=0, tiled=True)
    features = regrouped.shape[0]
    block_rows = regrouped.shape[1]
    local_width = features // groups
    score_scale = 1.0 / math.sqrt(features)
    inner_table = jnp.asarray(parity_table(local_width), jnp.bfloat16)
    outer_table = jnp.asarray(parity_table(groups), jnp.float32)
    blocked = regrouped.reshape(groups, local_width, block_rows)
    first_section = jnp.einsum(
        "abr,bc->acr", blocked, inner_table, preferred_element_type=jnp.float32
    )
    turned = (
        jnp.einsum("acr,ad->dcr", first_section, outer_table, precision=lax.Precision.HIGHEST)
        * score_scale
    )
    flattened = turned.reshape(features, block_rows)
    norm_factor = lax.rsqrt(jnp.mean(flattened * flattened, axis=0, keepdims=True) + 1e-06)
    unit_rows = (flattened * norm_factor).astype(jnp.bfloat16).T
    following = passed_along(unit_rows, "feat", -1)
    partner = from_partner(unit_rows, "rows", 0)
    following_partner = from_partner(following, "rows", 0)
    candidates = jnp.stack([unit_rows, following, partner, following_partner])
    tile_total = tile_blocks.shape[2]
    own_list = lax.dynamic_index_in_dim(tile_blocks[:, 0, :], row_place, 0, keepdims=False)
    own_count = lax.dynamic_index_in_dim(tile_counts[:, 0], row_place, 0, keepdims=False)

    def add_tile(slot_index, buffer):
        block_id = own_list[slot_index]
        other_half = (block_id // groups != row_place).astype(jnp.int32)
        other_bucket = (block_id % groups != feat_place).astype(jnp.int32)
        keyed_block = lax.dynamic_index_in_dim(
            candidates, other_bucket + 2 * other_half, 0, keepdims=False
        )
        tile_value = (
            lax.dot_general(
                unit_rows, keyed_block, (((1,), (1,)), ((), ())), preferred_element_type=jnp.float32
            )
            * score_scale
        )
        return lax.dynamic_update_index_in_dim(buffer, tile_value, slot_index, 0)

    empty_tiles = jnp.zeros((tile_total, block_rows, block_rows), jnp.float32)
    result = lax.fori_loop(0, own_count, add_tile, empty_tiles)
    return (result[None, None], unit_rows[None])


ACROSS = 2


def route_kernel(along, rows, emb_ref, signs_ref, *out_refs):
    place = lax.axis_index("feat")
    at = lax.div(place, ACROSS)
    side = lax.rem(place, ACROSS)
    step = emb_ref.shape[0]
    sign_row = signs_ref[pl.ds(pl.program_id(0), 1), :].astype(jnp.float32)
    sign_tile = jnp.broadcast_to(sign_row, (step, step)).T.astype(jnp.bfloat16)
    sign_wide = jnp.concatenate([sign_tile] * (rows // step), axis=1)
    for hop in range(along):
        there = lax.bitwise_xor(at, hop)
        first = ACROSS * there
        last = lax.rem(first + ACROSS, ACROSS * along)
        keep = jnp.where(side == 0, first, last)
        send = jnp.where(side == 0, last, first)
        for ref, block in (
            (out_refs[2 * hop], keep),
            (out_refs[2 * hop + 1].at[0], first + 1),
            (out_refs[2 * hop + 1].at[1], send),
        ):
            start = pl.multiple_of(block * rows, rows)
            ref[...] = emb_ref[:, pl.ds(start, rows)] * sign_wide


def route(embeddings, signs, along, rows):
    width, columns = embeddings.shape
    step = 128
    out_shape, out_specs = [], []
    for _ in range(along):
        out_shape += [
            jax.ShapeDtypeStruct((width, rows), jnp.bfloat16),
            jax.ShapeDtypeStruct((2, width, rows), jnp.bfloat16),
        ]
        out_specs += [
            pl.BlockSpec((step, rows), lambda i: (i, 0)),
            pl.BlockSpec((2, step, rows), lambda i: (0, i, 0)),
        ]
    return pl.pallas_call(
        functools.partial(route_kernel, along, rows),
        grid=(width // step,),
        in_specs=[
            pl.BlockSpec((step, columns), lambda i: (i, 0)),
            pl.BlockSpec((width // step, step), lambda i: (0, 0)),
        ],
        out_specs=out_specs,
        out_shape=out_shape,
        compiler_params=pltpu.CompilerParams(vmem_limit_bytes=VMEM_LIMIT),
        cost_estimate=pl.CostEstimate(flops=width * columns, bytes_accessed=5 << 20, transcendentals=0),
        name="route",
    )(embeddings, signs.reshape(width // step, step))


def butterfly(parts):
    parts = list(parts)
    half = 1
    while half < len(parts):
        for low in range(0, len(parts), 2 * half):
            for i in range(low, low + half):
                a, b = parts[i], parts[i + half]
                parts[i], parts[i + half] = a + b, a - b
        half *= 2
    return parts


def rotate_kernel(picks, *refs):
    count = len(picks)
    piece_refs, table_ref, out_ref = refs[:count], refs[count], refs[count + 1]
    pieces, turned, sems = refs[count + 2 :]
    copies = []
    for i, pick in enumerate(picks):
        source = piece_refs[i] if pick is None else piece_refs[i].at[pick]
        copies.append(pltpu.make_async_copy(source, pieces.at[i], sems.at[i]))
    for copy in copies:
        copy.start()
    place = lax.axis_index("feat")
    width, rows = pieces.shape[1:]
    features = count * width
    chunk = 256
    total = jnp.zeros((rows, 128), jnp.float32)
    for copy in copies:
        copy.wait()
    for low in range(0, width, chunk):
        parts = butterfly(
            lax.dot_general(
                pieces[i],
                table_ref[:, low : low + chunk],
                (((0,), (0,)), ((), ())),
                preferred_element_type=jnp.float32,
            )
            for i in range(count)
        )
        for i, part in enumerate(parts):
            turned[:, i * width + low : i * width + low + chunk] = part
            square = part * part
            for lane in range(0, chunk, 128):
                total = total + square[:, lane : lane + 128]
    mean = jnp.sum(total, axis=1, keepdims=True) * (1.0 / (features * features))
    factor = lax.rsqrt(mean + 1e-06) * (1.0 / math.sqrt(features))
    for i in range(count):
        odd = jnp.int32(0)
        for bit in range(count.bit_length() - 1):
            if i >> bit & 1:
                odd = odd + (lax.shift_right_logical(place, bit) & 1)
        sign = (1 - 2 * (odd & 1)).astype(jnp.float32)
        columns = slice(i * width, (i + 1) * width)
        out_ref[:, columns] = (turned[:, columns] * (factor * sign)).astype(jnp.bfloat16)


def rotate(pieces, picks, table):
    count = len(pieces)
    width, rows = pieces[0].shape[-2:]
    return pl.pallas_call(
        functools.partial(rotate_kernel, picks),
        in_specs=[ANY] * count + [pl.BlockSpec(memory_space=pltpu.VMEM)],
        out_specs=pl.BlockSpec(memory_space=pltpu.VMEM),
        out_shape=jax.ShapeDtypeStruct((rows, count * width), jnp.bfloat16),
        scratch_shapes=[
            pltpu.VMEM((count, width, rows), jnp.bfloat16),
            pltpu.VMEM((rows, count * width), jnp.float32),
            pltpu.SemaphoreType.DMA((count,)),
        ],
        compiler_params=pltpu.CompilerParams(vmem_limit_bytes=VMEM_LIMIT),
        cost_estimate=pl.CostEstimate(
            flops=2 * rows * count * width * width, bytes_accessed=5 << 20, transcendentals=0
        ),
        name="rotate",
    )(*pieces, table)


def listed(lists_ref, counts_ref, slot, groups):
    place = lax.axis_index("feat")
    half = lax.axis_index("rows")
    block_id = lists_ref[half, slot]
    other_half = (lax.div(block_id, groups) != half).astype(jnp.int32)
    own_bucket = (lax.rem(block_id, groups) == place).astype(jnp.int32)
    side = lax.rem(place, ACROSS)
    is_outer = (own_bucket != side).astype(jnp.int32)
    choice = is_outer + 2 * other_half
    return jnp.where(slot < counts_ref[half], choice, -1)


def product(query, key, features):
    return lax.dot_general(
        query, key, (((1,), (1,)), ((), ())), preferred_element_type=jnp.float32
    ) * (1.0 / math.sqrt(features))


def early_kernel(groups, lists_ref, counts_ref, mid_ref, outer_ref, mid2_ref, tiles_ref, unit_ref, blocks, sems, out_sem):
    copies = [
        pltpu.make_async_copy(ref, blocks.at[i], sems.at[i])
        for i, ref in enumerate((mid_ref, outer_ref, mid2_ref))
    ]
    for copy in copies:
        copy.start()
    for copy in copies:
        copy.wait()
    own = 1 - lax.rem(lax.axis_index("feat"), ACROSS)
    out = pltpu.make_async_copy(blocks.at[own], unit_ref, out_sem)
    out.start()
    features = blocks.shape[2]
    for slot in range(tiles_ref.shape[0]):
        choice = listed(lists_ref, counts_ref, slot, groups)
        wanted = (choice >= 0) & (choice < 3)

        @pl.when(wanted)
        def _():
            tiles_ref[slot] = product(blocks[own], blocks[jnp.clip(choice, 0, 2)], features)

        @pl.when(jnp.logical_not(wanted))
        def _():
            tiles_ref[slot] = jnp.zeros(tiles_ref.shape[1:], jnp.float32)

    out.wait()


def late_kernel(groups, lists_ref, counts_ref, unit_ref, outer2_ref, early_ref, tiles_ref, blocks, tile, sems, out_sem):
    features = blocks.shape[2]
    choices = [listed(lists_ref, counts_ref, slot, groups) for slot in range(early_ref.shape[0])]
    needed = functools.reduce(jnp.logical_or, [choice == 3 for choice in choices])
    slot = jnp.int32(0)
    for i, choice in enumerate(choices):
        slot = jnp.where(choice == 3, i, slot)

    @pl.when(needed)
    def _():
        copies = [
            pltpu.make_async_copy(ref, blocks.at[i], sems.at[i])
            for i, ref in enumerate((unit_ref, outer2_ref))
        ]
        for copy in copies:
            copy.start()
        for copy in copies:
            copy.wait()
        tile[...] = product(blocks[0], blocks[1], features)
        out = pltpu.make_async_copy(tile, tiles_ref.at[slot], out_sem)
        out.start()
        out.wait()


def scores_early(lists, counts, mid, outer, mid2, groups):
    rows, features = mid.shape
    tiles = lists.shape[1]
    return pl.pallas_call(
        functools.partial(early_kernel, groups),
        in_specs=[SMEM, SMEM, ANY, ANY, ANY],
        out_specs=[pl.BlockSpec(memory_space=pltpu.VMEM), ANY],
        out_shape=[
            jax.ShapeDtypeStruct((tiles, rows, rows), jnp.float32),
            jax.ShapeDtypeStruct((rows, features), jnp.bfloat16),
        ],
        scratch_shapes=[
            pltpu.VMEM((3, rows, features), jnp.bfloat16),
            pltpu.SemaphoreType.DMA((3,)),
            pltpu.SemaphoreType.DMA,
        ],
        compiler_params=pltpu.CompilerParams(vmem_limit_bytes=VMEM_LIMIT),
        cost_estimate=pl.CostEstimate(
            flops=4 * rows * rows * features, bytes_accessed=9 << 20, transcendentals=0
        ),
        name="early",
    )(lists, counts, mid, outer, mid2)


def scores_late(lists, counts, unit, outer2, early, groups):
    rows, features = unit.shape
    return pl.pallas_call(
        functools.partial(late_kernel, groups),
        in_specs=[SMEM, SMEM, ANY, ANY, ANY],
        out_specs=ANY,
        out_shape=jax.ShapeDtypeStruct(early.shape, early.dtype),
        scratch_shapes=[
            pltpu.VMEM((2, rows, features), jnp.bfloat16),
            pltpu.VMEM((rows, rows), jnp.float32),
            pltpu.SemaphoreType.DMA((2,)),
            pltpu.SemaphoreType.DMA,
        ],
        input_output_aliases={4: 0},
        compiler_params=pltpu.CompilerParams(vmem_limit_bytes=VMEM_LIMIT),
        cost_estimate=pl.CostEstimate(
            flops=2 * rows * rows * features, bytes_accessed=4 << 20, transcendentals=0
        ),
        name="late",
    )(lists, counts, unit, outer2, early)


def hop_over(value, axis, mask):
    count = lax.axis_size(axis)
    return lax.ppermute(value, axis, [(i, i ^ mask) for i in range(count)])


def paired(embeddings, signs, tile_blocks, tile_counts):
    groups = lax.axis_size("feat")
    along = groups // ACROSS
    width, columns = embeddings.shape
    rows = columns // groups
    table = jnp.asarray(parity_table(width), jnp.bfloat16)
    routed = route(embeddings, signs, along, rows)
    kept, shared = [routed[0]], [routed[1]]
    for hop in range(1, along):
        shared.append(hop_over(routed[2 * hop + 1], "feat", ACROSS * hop))
        kept.append(hop_over(routed[2 * hop], "feat", ACROSS * hop))
    crossed = [hop_over(value, "feat", 1) for value in shared]
    mid_pieces, mid_picks, outer_pieces, outer_picks = [], [], [], []
    for hop in range(along):
        mid_pieces += [shared[hop], crossed[hop]]
        mid_picks += [0, 0]
        outer_pieces += [kept[hop], crossed[hop]]
        outer_picks += [None, 1]
    mid = rotate(mid_pieces, mid_picks, table)
    mid2 = hop_over(mid, "rows", 1)
    outer = rotate(outer_pieces, outer_picks, table)
    outer2 = hop_over(outer, "rows", 1)
    lists = tile_blocks[:, 0, :]
    counts = tile_counts[:, 0]
    early, unit = scores_early(lists, counts, mid, outer, mid2, groups)
    tiles = scores_late(lists, counts, unit, outer2, early, groups)
    return (tiles[None, None], unit[None])


def solution(mesh):
    body = paired if mesh.shape["feat"] == 8 and mesh.shape["rows"] == 2 else general
    return jax.shard_map(
        body,
        mesh=mesh,
        in_specs=(
            P("feat", ("groups", "rows")),
            P("feat"),
            P("groups", "feat", None),
            P("groups", "feat"),
        ),
        out_specs=(
            P(("groups", "rows"), "feat", None, None, None),
            P(("groups", "rows"), "feat", None),
        ),
        check_vma=False,
    )
```

```python
import functools
import math

import jax
import jax.numpy as jnp
import numpy as np
from jax import lax
from jax.experimental import pallas as pl
from jax.experimental.pallas import tpu as pltpu
from jax.sharding import PartitionSpec as P

SMEM = pl.BlockSpec(memory_space=pltpu.SMEM)
VMEM = pl.BlockSpec(memory_space=pltpu.VMEM)
HBM = pl.BlockSpec(memory_space=pltpu.HBM)
VMEM_LIMIT = 24 << 20


def parity_table(length):
    positions = np.arange(length)
    shared = positions[:, None] & positions[None, :]
    parity = np.zeros_like(shared)
    while shared.any():
        parity ^= shared & 1
        shared = shared >> 1
    return 1 - 2 * parity


def from_partner(block, axis, distance):
    count = lax.axis_size(axis)
    route = []
    for low in range(count):
        high = low | 1 << distance
        if high != low and high < count:
            route += [(low, high), (high, low)]
    return lax.ppermute(block, axis, route)


def passed_along(value, axis, steps):
    count = lax.axis_size(axis)
    pairs = [(source, (source + steps) % count) for source in range(count)]
    return lax.ppermute(value, axis, pairs)


def general(embeddings, signs, tile_blocks, tile_counts):
    groups = lax.axis_size("feat")
    feat_place = lax.axis_index("feat")
    row_place = lax.axis_index("rows")
    signed = embeddings * signs.astype(jnp.bfloat16)[:, None]
    regrouped = lax.all_to_all(signed, "feat", split_axis=1, concat_axis=0, tiled=True)
    features = regrouped.shape[0]
    block_rows = regrouped.shape[1]
    local_width = features // groups
    score_scale = 1.0 / math.sqrt(features)
    inner_table = jnp.asarray(parity_table(local_width), jnp.bfloat16)
    outer_table = jnp.asarray(parity_table(groups), jnp.float32)
    blocked = regrouped.reshape(groups, local_width, block_rows)
    first_section = jnp.einsum(
        "abr,bc->acr", blocked, inner_table, preferred_element_type=jnp.float32
    )
    turned = (
        jnp.einsum("acr,ad->dcr", first_section, outer_table, precision=lax.Precision.HIGHEST)
        * score_scale
    )
    flattened = turned.reshape(features, block_rows)
    norm_factor = lax.rsqrt(jnp.mean(flattened * flattened, axis=0, keepdims=True) + 1e-06)
    unit_rows = (flattened * norm_factor).astype(jnp.bfloat16).T
    following = passed_along(unit_rows, "feat", -1)
    partner = from_partner(unit_rows, "rows", 0)
    following_partner = from_partner(following, "rows", 0)
    candidates = jnp.stack([unit_rows, following, partner, following_partner])
    tile_total = tile_blocks.shape[2]
    own_list = lax.dynamic_index_in_dim(tile_blocks[:, 0, :], row_place, 0, keepdims=False)
    own_count = lax.dynamic_index_in_dim(tile_counts[:, 0], row_place, 0, keepdims=False)

    def add_tile(slot_index, buffer):
        block_id = own_list[slot_index]
        other_half = (block_id // groups != row_place).astype(jnp.int32)
        other_bucket = (block_id % groups != feat_place).astype(jnp.int32)
        keyed_block = lax.dynamic_index_in_dim(
            candidates, other_bucket + 2 * other_half, 0, keepdims=False
        )
        tile_value = (
            lax.dot_general(
                unit_rows, keyed_block, (((1,), (1,)), ((), ())), preferred_element_type=jnp.float32
            )
            * score_scale
        )
        return lax.dynamic_update_index_in_dim(buffer, tile_value, slot_index, 0)

    empty_tiles = jnp.zeros((tile_total, block_rows, block_rows), jnp.float32)
    result = lax.fori_loop(0, own_count, add_tile, empty_tiles)
    return (result[None, None], unit_rows[None])


ACROSS = 2
ALONG = 4


def signs_kernel(signs_ref, wide_ref):
    step = signs_ref.shape[1]
    for i in range(signs_ref.shape[0]):
        tile = jnp.broadcast_to(signs_ref[i : i + 1, :].astype(jnp.float32), (step, step))
        tile = tile.T.astype(jnp.bfloat16)
        for low in range(0, wide_ref.shape[1], step):
            wide_ref[i * step : (i + 1) * step, low : low + step] = tile


def wanted(hop):
    place = lax.axis_index("feat")
    side = lax.rem(place, ACROSS)
    first = ACROSS * lax.bitwise_xor(lax.div(place, ACROSS), hop)
    last = lax.rem(first + ACROSS, ACROSS * ALONG)
    return jnp.where(side == 0, first, last), first + 1, jnp.where(side == 0, last, first)


def route_kernel(emb_ref, signs_ref, *refs):
    out_refs, (sign_rows, wide_ref, sign_sem, sems) = list(refs[:-4]), refs[-4:]
    sign_copy = pltpu.make_async_copy(signs_ref, sign_rows, sign_sem)
    sign_copy.start()
    targets = []
    for hop in range(ALONG):
        kept, middle, other = wanted(hop)
        targets.append((out_refs.pop(0), kept))
        if hop == ALONG - 1:
            targets += [(out_refs.pop(0), middle), (out_refs.pop(0), other)]
        else:
            shared = out_refs.pop(0)
            targets += [(shared.at[0], middle), (shared.at[1], other)]
    copies = []
    for i, (ref, block) in enumerate(targets):
        rows = ref.shape[1]
        start = pl.multiple_of(block * rows, rows)
        copies.append(pltpu.make_async_copy(emb_ref.at[:, pl.ds(start, rows)], ref, sems.at[i]))
    for copy in copies:
        copy.start()
    sign_copy.wait()
    signs_kernel(sign_rows, wide_ref)
    for copy, (ref, block) in zip(copies, targets):
        copy.wait()
        ref[...] = ref[...] * wide_ref[...]


def route(embeddings, signs, rows):
    width = embeddings.shape[0]
    one = jax.ShapeDtypeStruct((width, rows), jnp.bfloat16)
    two = jax.ShapeDtypeStruct((2, width, rows), jnp.bfloat16)
    out_shape = [one, two] * (ALONG - 1) + [one] * 3
    sign_rows = signs.reshape(width // 128, 128)
    return pl.pallas_call(
        route_kernel,
        in_specs=[HBM, HBM],
        out_specs=[VMEM] * len(out_shape),
        out_shape=out_shape,
        scratch_shapes=[
            pltpu.VMEM(sign_rows.shape, sign_rows.dtype),
            pltpu.VMEM((width, rows), jnp.bfloat16),
            pltpu.SemaphoreType.DMA,
            pltpu.SemaphoreType.DMA((3 * ALONG,)),
        ],
        compiler_params=pltpu.CompilerParams(vmem_limit_bytes=VMEM_LIMIT),
        cost_estimate=pl.CostEstimate(
            flops=3 * ALONG * width * rows,
            bytes_accessed=3 * ALONG * width * rows * 4,
            transcendentals=0,
        ),
        name="route",
    )(*(pltpu.with_memory_space_constraint(value, pltpu.HBM) for value in (embeddings, sign_rows)))


def butterfly(parts):
    parts = list(parts)
    half = 1
    while half < len(parts):
        for low in range(0, len(parts), 2 * half):
            for i in range(low, low + half):
                a, b = parts[i], parts[i + half]
                parts[i], parts[i + half] = a + b, a - b
        half *= 2
    return parts


def rotate_kernel(picks, *refs):
    count = len(picks)
    table_ref, out_ref, turned = refs[-3:]
    place = lax.axis_index("feat")
    pieces = [pick(refs, place) for pick in picks]
    width, rows = pieces[0].shape
    features = count * width
    chunk = 256
    total = jnp.zeros((rows, 128), jnp.float32)
    for low in range(0, width, chunk):
        parts = butterfly(
            lax.dot_general(
                piece,
                table_ref[:, low : low + chunk],
                (((0,), (0,)), ((), ())),
                preferred_element_type=jnp.float32,
            )
            for piece in pieces
        )
        for i, part in enumerate(parts):
            turned[:, i * width + low : i * width + low + chunk] = part
            square = part * part
            for lane in range(0, chunk, 128):
                total = total + square[:, lane : lane + 128]
    mean = jnp.sum(total, axis=1, keepdims=True) * (1.0 / (features * features))
    factor = lax.rsqrt(mean + 1e-06) * (1.0 / math.sqrt(features))
    for i in range(count):
        odd = jnp.int32(0)
        for bit in range(count.bit_length() - 1):
            if i >> bit & 1:
                odd = odd + (lax.shift_right_logical(place, bit) & 1)
        sign = (1 - 2 * (odd & 1)).astype(jnp.float32)
        columns = slice(i * width, (i + 1) * width)
        out_ref[:, columns] = (turned[:, columns] * (factor * sign)).astype(jnp.bfloat16)


def rotate(inputs, picks, table):
    count = len(picks)
    width, rows = inputs[0].shape[-2:]
    return pl.pallas_call(
        functools.partial(rotate_kernel, picks),
        in_specs=[VMEM] * (len(inputs) + 1),
        out_specs=VMEM,
        out_shape=jax.ShapeDtypeStruct((rows, count * width), jnp.bfloat16),
        scratch_shapes=[pltpu.VMEM((rows, count * width), jnp.float32)],
        compiler_params=pltpu.CompilerParams(vmem_limit_bytes=VMEM_LIMIT),
        cost_estimate=pl.CostEstimate(
            flops=2 * rows * count * width * width, bytes_accessed=5 << 20, transcendentals=0
        ),
        name="rotate",
    )(*inputs, table)


def listed(lists_ref, counts_ref, slot, groups):
    place = lax.axis_index("feat")
    half = lax.axis_index("rows")
    block_id = lists_ref[half, slot]
    other_half = (lax.div(block_id, groups) != half).astype(jnp.int32)
    own_bucket = (lax.rem(block_id, groups) == place).astype(jnp.int32)
    side = lax.rem(place, ACROSS)
    is_outer = (own_bucket != side).astype(jnp.int32)
    choice = is_outer + 2 * other_half
    return jnp.where(slot < counts_ref[half], choice, -1)


def product(query, key, features):
    return lax.dot_general(
        query, key, (((1,), (1,)), ((), ())), preferred_element_type=jnp.float32
    ) * (1.0 / math.sqrt(features))


def early_kernel(groups, lists_ref, counts_ref, mid_ref, outer_ref, mid2_ref, tiles_ref, unit_ref, out_sem):
    own_middle = lax.rem(lax.axis_index("feat"), ACROSS) == 1
    features = mid_ref.shape[1]
    keys = (mid_ref, outer_ref, mid2_ref)
    for value, query_ref in ((True, mid_ref), (False, outer_ref)):

        @pl.when(own_middle == value)
        def _(query_ref=query_ref):
            pltpu.make_async_copy(query_ref, unit_ref, out_sem).start()

    def fill(slot, carry):
        choice = listed(lists_ref, counts_ref, slot, groups)

        @pl.when((choice < 0) | (choice > 2))
        def _():
            tiles_ref[slot] = jnp.zeros(tiles_ref.shape[1:], jnp.float32)

        for value, query_ref in ((True, mid_ref), (False, outer_ref)):
            for index, key_ref in enumerate(keys):

                @pl.when((own_middle == value) & (choice == index))
                def _(query_ref=query_ref, key_ref=key_ref):
                    tiles_ref[slot] = product(query_ref[...], key_ref[...], features)

        return carry

    lax.fori_loop(0, tiles_ref.shape[0], fill, 0)
    pltpu.make_async_copy(mid_ref, unit_ref, out_sem).wait()


def late_kernel(groups, lists_ref, counts_ref, mid_ref, outer_ref, outer2_ref, early_ref, tiles_ref, tile, out_sem):
    own_middle = lax.rem(lax.axis_index("feat"), ACROSS) == 1
    features = mid_ref.shape[1]
    choices = [listed(lists_ref, counts_ref, slot, groups) for slot in range(early_ref.shape[0])]
    needed = functools.reduce(jnp.logical_or, [choice == 3 for choice in choices])
    slot = jnp.int32(0)
    for i, choice in enumerate(choices):
        slot = jnp.where(choice == 3, i, slot)
    for value, query_ref in ((True, mid_ref), (False, outer_ref)):

        @pl.when((own_middle == value) & needed)
        def _(query_ref=query_ref):
            tile[...] = product(query_ref[...], outer2_ref[...], features)

    @pl.when(needed)
    def _():
        out = pltpu.make_async_copy(tile, tiles_ref.at[slot], out_sem)
        out.start()
        out.wait()


def scores_early(lists, counts, mid, outer, mid2, groups):
    rows, features = mid.shape
    tiles = lists.shape[1]
    return pl.pallas_call(
        functools.partial(early_kernel, groups),
        in_specs=[SMEM, SMEM, VMEM, VMEM, VMEM],
        out_specs=[VMEM, HBM],
        out_shape=[
            jax.ShapeDtypeStruct((tiles, rows, rows), jnp.float32),
            jax.ShapeDtypeStruct((rows, features), jnp.bfloat16),
        ],
        scratch_shapes=[pltpu.SemaphoreType.DMA],
        compiler_params=pltpu.CompilerParams(vmem_limit_bytes=VMEM_LIMIT),
        cost_estimate=pl.CostEstimate(
            flops=4 * rows * rows * features, bytes_accessed=9 << 20, transcendentals=0
        ),
        name="early",
    )(lists, counts, mid, outer, mid2)


def scores_late(lists, counts, mid, outer, outer2, early, groups):
    rows, features = mid.shape
    return pl.pallas_call(
        functools.partial(late_kernel, groups),
        in_specs=[SMEM, SMEM, VMEM, VMEM, VMEM, HBM],
        out_specs=HBM,
        out_shape=jax.ShapeDtypeStruct(early.shape, early.dtype),
        scratch_shapes=[pltpu.VMEM((rows, rows), jnp.float32), pltpu.SemaphoreType.DMA],
        input_output_aliases={5: 0},
        compiler_params=pltpu.CompilerParams(vmem_limit_bytes=VMEM_LIMIT),
        cost_estimate=pl.CostEstimate(
            flops=2 * rows * rows * features, bytes_accessed=4 << 20, transcendentals=0
        ),
        name="late",
    )(lists, counts, mid, outer, outer2, early)


ORDER = "S2 O3 X0 S1 X1 X2 K1:X0 R2 B3:S2 K2:X1 K3:X1 XO:R2 R3:R2,K2,K3 XB:K1".split()


def after(value, *events):
    return lax.optimization_barrier((value, *events))[0]


def chip(at, side):
    return ACROSS * at + side


EVERY = tuple(range(ACROSS * ALONG))
DIRECT = (chip(0, 0), chip(1, 1), chip(2, 0), chip(3, 1))
RELAYED = (chip(1, 0), chip(0, 1), chip(3, 0), chip(2, 1))
NEAR = 1
FAR = (2, 3)


def hop_over(value, axis, mask, receivers=None):
    if receivers is None:
        receivers = range(lax.axis_size(axis))
    return lax.ppermute(value, axis, [(to ^ mask, to) for to in receivers])


def along(value, hop, receivers=EVERY):
    return hop_over(value, "feat", ACROSS * hop, receivers)


def across(value):
    return hop_over(value, "feat", 1)


def plain(index, pick=None):
    if pick is None:
        return lambda refs, place: refs[index][...]
    return lambda refs, place: refs[index][pick]


def kept_far(direct, relayed):
    def read(refs, place):
        straight = lax.rem(lax.div(place, ACROSS) + lax.rem(place, ACROSS), 2) == 0
        return jnp.where(straight, refs[direct][...], refs[relayed][...])

    return read


def paired(embeddings, signs, tile_blocks, tile_counts):
    groups = lax.axis_size("feat")
    width, columns = embeddings.shape
    rows = columns // groups
    table = jnp.asarray(parity_table(width), jnp.bfloat16)
    K0, S0, K1, S1, K2, S2, K3, B3, O3 = route(embeddings, signs, rows)
    plan = {
        "S1": lambda got: (S1, along, 1),
        "S2": lambda got: (S2, along, 2),
        "B3": lambda got: (B3, along, 3),
        "O3": lambda got: (O3, along, 3),
        "K1": lambda got: (K1, along, 1),
        "K2": lambda got: (K2, along, 2, DIRECT),
        "K3": lambda got: (K3, along, 3, DIRECT),
        "X0": lambda got: (S0, across),
        "X1": lambda got: (got["S1"], across),
        "X2": lambda got: (got["S2"], across),
        "XB": lambda got: (got["B3"], across),
        "XO": lambda got: (got["O3"], across),
        "R2": lambda got: (got["S2"][1], along, NEAR, RELAYED),
        "R3": lambda got: (got["O3"], along, NEAR, RELAYED),
    }
    got = {}
    for entry in ORDER:
        name, _, events = entry.partition(":")
        value, move, *rest = plan[name](got)
        if events:
            value = after(value, *(got[event] for event in events.split(",")))
        with jax.named_scope(name):
            got[name] = move(value, *rest)
    mid = rotate(
        [S0, got["X0"], got["S1"], got["X1"], got["S2"], got["X2"], got["B3"], got["XB"]],
        [plain(i, 0 if i < 6 else None) for i in range(8)],
        table,
    )
    mid2 = hop_over(mid, "rows", 1)
    outer = rotate(
        [K0, got["X0"], got["K1"], got["X1"], got["K2"], got["R3"], got["X2"], got["K3"], got["R2"], got["XO"]],
        [plain(0), plain(1, 1), plain(2), plain(3, 1), kept_far(4, 5), plain(6, 1), kept_far(7, 8), plain(9)],
        table,
    )
    outer2 = hop_over(outer, "rows", 1)
    lists = tile_blocks[:, 0, :]
    counts = tile_counts[:, 0]
    early, unit = scores_early(lists, counts, mid, outer, mid2, groups)
    tiles = scores_late(lists, counts, mid, outer, outer2, early, groups)
    return (tiles[None, None], unit[None])


def solution(mesh):
    body = paired if mesh.shape["feat"] == ALONG * ACROSS and mesh.shape["rows"] == 2 else general
    return jax.shard_map(
        body,
        mesh=mesh,
        in_specs=(
            P("feat", ("groups", "rows")),
            P("feat"),
            P("groups", "feat", None),
            P("groups", "feat"),
        ),
        out_specs=(
            P(("groups", "rows"), "feat", None, None, None),
            P(("groups", "rows"), "feat", None),
        ),
        check_vma=False,
    )
```

```python
import functools
import math

import jax
import jax.numpy as jnp
import numpy as np
from jax import lax
from jax.experimental import pallas as pl
from jax.experimental.pallas import tpu as pltpu
from jax.sharding import PartitionSpec as P

SMEM = pl.BlockSpec(memory_space=pltpu.SMEM)
VMEM = pl.BlockSpec(memory_space=pltpu.VMEM)
HBM = pl.BlockSpec(memory_space=pltpu.HBM)
VMEM_LIMIT = 24 << 20


def parity_table(length):
    positions = np.arange(length)
    shared = positions[:, None] & positions[None, :]
    parity = np.zeros_like(shared)
    while shared.any():
        parity ^= shared & 1
        shared = shared >> 1
    return 1 - 2 * parity


def from_partner(block, axis, distance):
    count = lax.axis_size(axis)
    route = []
    for low in range(count):
        high = low | 1 << distance
        if high != low and high < count:
            route += [(low, high), (high, low)]
    return lax.ppermute(block, axis, route)


def passed_along(value, axis, steps):
    count = lax.axis_size(axis)
    pairs = [(source, (source + steps) % count) for source in range(count)]
    return lax.ppermute(value, axis, pairs)


def general(embeddings, signs, tile_blocks, tile_counts):
    groups = lax.axis_size("feat")
    feat_place = lax.axis_index("feat")
    row_place = lax.axis_index("rows")
    signed = embeddings * signs.astype(jnp.bfloat16)[:, None]
    regrouped = lax.all_to_all(signed, "feat", split_axis=1, concat_axis=0, tiled=True)
    features = regrouped.shape[0]
    block_rows = regrouped.shape[1]
    local_width = features // groups
    score_scale = 1.0 / math.sqrt(features)
    inner_table = jnp.asarray(parity_table(local_width), jnp.bfloat16)
    outer_table = jnp.asarray(parity_table(groups), jnp.float32)
    blocked = regrouped.reshape(groups, local_width, block_rows)
    first_section = jnp.einsum(
        "abr,bc->acr", blocked, inner_table, preferred_element_type=jnp.float32
    )
    turned = (
        jnp.einsum("acr,ad->dcr", first_section, outer_table, precision=lax.Precision.HIGHEST)
        * score_scale
    )
    flattened = turned.reshape(features, block_rows)
    norm_factor = lax.rsqrt(jnp.mean(flattened * flattened, axis=0, keepdims=True) + 1e-06)
    unit_rows = (flattened * norm_factor).astype(jnp.bfloat16).T
    following = passed_along(unit_rows, "feat", -1)
    partner = from_partner(unit_rows, "rows", 0)
    following_partner = from_partner(following, "rows", 0)
    candidates = jnp.stack([unit_rows, following, partner, following_partner])
    tile_total = tile_blocks.shape[2]
    own_list = lax.dynamic_index_in_dim(tile_blocks[:, 0, :], row_place, 0, keepdims=False)
    own_count = lax.dynamic_index_in_dim(tile_counts[:, 0], row_place, 0, keepdims=False)

    def add_tile(slot_index, buffer):
        block_id = own_list[slot_index]
        other_half = (block_id // groups != row_place).astype(jnp.int32)
        other_bucket = (block_id % groups != feat_place).astype(jnp.int32)
        keyed_block = lax.dynamic_index_in_dim(
            candidates, other_bucket + 2 * other_half, 0, keepdims=False
        )
        tile_value = (
            lax.dot_general(
                unit_rows, keyed_block, (((1,), (1,)), ((), ())), preferred_element_type=jnp.float32
            )
            * score_scale
        )
        return lax.dynamic_update_index_in_dim(buffer, tile_value, slot_index, 0)

    empty_tiles = jnp.zeros((tile_total, block_rows, block_rows), jnp.float32)
    result = lax.fori_loop(0, own_count, add_tile, empty_tiles)
    return (result[None, None], unit_rows[None])


ACROSS = 2
ALONG = 4


def signs_kernel(signs_ref, wide_ref):
    step = signs_ref.shape[1]
    for i in range(signs_ref.shape[0]):
        tile = jnp.broadcast_to(signs_ref[i : i + 1, :].astype(jnp.float32), (step, step))
        tile = tile.T.astype(jnp.bfloat16)
        for low in range(0, wide_ref.shape[1], step):
            wide_ref[i * step : (i + 1) * step, low : low + step] = tile


def wanted(hop):
    place = lax.axis_index("feat")
    side = lax.rem(place, ACROSS)
    first = ACROSS * lax.bitwise_xor(lax.div(place, ACROSS), hop)
    last = lax.rem(first + ACROSS, ACROSS * ALONG)
    return jnp.where(side == 0, first, last), first + 1, jnp.where(side == 0, last, first)


def route_kernel(emb_ref, signs_ref, *refs):
    out_refs, (sign_rows, wide_ref, sign_sem, sems) = list(refs[:-4]), refs[-4:]
    sign_copy = pltpu.make_async_copy(signs_ref, sign_rows, sign_sem)
    sign_copy.start()
    targets = []
    for hop in range(ALONG):
        kept, middle, other = wanted(hop)
        targets.append((out_refs.pop(0), kept))
        if hop == ALONG - 1:
            targets += [(out_refs.pop(0), middle), (out_refs.pop(0), other)]
        else:
            shared = out_refs.pop(0)
            targets += [(shared.at[0], middle), (shared.at[1], other)]
    copies = []
    for i, (ref, block) in enumerate(targets):
        rows = ref.shape[1]
        start = pl.multiple_of(block * rows, rows)
        copies.append(pltpu.make_async_copy(emb_ref.at[:, pl.ds(start, rows)], ref, sems.at[i]))
    for copy in copies:
        copy.start()
    sign_copy.wait()
    signs_kernel(sign_rows, wide_ref)
    for copy, (ref, block) in zip(copies, targets):
        copy.wait()
        ref[...] = ref[...] * wide_ref[...]


def route(embeddings, signs, rows):
    width = embeddings.shape[0]
    one = jax.ShapeDtypeStruct((width, rows), jnp.bfloat16)
    two = jax.ShapeDtypeStruct((2, width, rows), jnp.bfloat16)
    out_shape = [one, two] * (ALONG - 1) + [one] * 3
    sign_rows = signs.reshape(width // 128, 128)
    return pl.pallas_call(
        route_kernel,
        in_specs=[HBM, HBM],
        out_specs=[VMEM] * len(out_shape),
        out_shape=out_shape,
        scratch_shapes=[
            pltpu.VMEM(sign_rows.shape, sign_rows.dtype),
            pltpu.VMEM((width, rows), jnp.bfloat16),
            pltpu.SemaphoreType.DMA,
            pltpu.SemaphoreType.DMA((3 * ALONG,)),
        ],
        compiler_params=pltpu.CompilerParams(vmem_limit_bytes=VMEM_LIMIT),
        cost_estimate=pl.CostEstimate(
            flops=3 * ALONG * width * rows,
            bytes_accessed=3 * ALONG * width * rows * 4,
            transcendentals=0,
        ),
        name="route",
    )(*(pltpu.with_memory_space_constraint(value, pltpu.HBM) for value in (embeddings, sign_rows)))


def butterfly(parts):
    parts = list(parts)
    half = 1
    while half < len(parts):
        for low in range(0, len(parts), 2 * half):
            for i in range(low, low + half):
                a, b = parts[i], parts[i + half]
                parts[i], parts[i + half] = a + b, a - b
        half *= 2
    return parts


def rotate_kernel(picks, *refs):
    count = len(picks)
    table_ref, out_ref, turned = refs[-3:]
    place = lax.axis_index("feat")
    pieces = [pick(refs, place) for pick in picks]
    width, rows = pieces[0].shape
    features = count * width
    chunk = 256
    total = jnp.zeros((rows, 128), jnp.float32)
    for low in range(0, width, chunk):
        parts = butterfly(
            lax.dot_general(
                piece,
                table_ref[:, low : low + chunk],
                (((0,), (0,)), ((), ())),
                preferred_element_type=jnp.float32,
            )
            for piece in pieces
        )
        for i, part in enumerate(parts):
            turned[:, i * width + low : i * width + low + chunk] = part
            square = part * part
            for lane in range(0, chunk, 128):
                total = total + square[:, lane : lane + 128]
    mean = jnp.sum(total, axis=1, keepdims=True) * (1.0 / (features * features))
    factor = lax.rsqrt(mean + 1e-06) * (1.0 / math.sqrt(features))
    for i in range(count):
        odd = jnp.int32(0)
        for bit in range(count.bit_length() - 1):
            if i >> bit & 1:
                odd = odd + (lax.shift_right_logical(place, bit) & 1)
        sign = (1 - 2 * (odd & 1)).astype(jnp.float32)
        columns = slice(i * width, (i + 1) * width)
        out_ref[:, columns] = (turned[:, columns] * (factor * sign)).astype(jnp.bfloat16)


def rotate(inputs, picks, table):
    count = len(picks)
    width, rows = inputs[0].shape[-2:]
    return pl.pallas_call(
        functools.partial(rotate_kernel, picks),
        in_specs=[VMEM] * (len(inputs) + 1),
        out_specs=VMEM,
        out_shape=jax.ShapeDtypeStruct((rows, count * width), jnp.bfloat16),
        scratch_shapes=[pltpu.VMEM((rows, count * width), jnp.float32)],
        compiler_params=pltpu.CompilerParams(vmem_limit_bytes=VMEM_LIMIT),
        cost_estimate=pl.CostEstimate(
            flops=2 * rows * count * width * width, bytes_accessed=5 << 20, transcendentals=0
        ),
        name="rotate",
    )(*inputs, table)


def listed(lists_ref, counts_ref, slot, groups):
    place = lax.axis_index("feat")
    half = lax.axis_index("rows")
    block_id = lists_ref[half, slot]
    other_half = (lax.div(block_id, groups) != half).astype(jnp.int32)
    own_bucket = (lax.rem(block_id, groups) == place).astype(jnp.int32)
    side = lax.rem(place, ACROSS)
    is_outer = (own_bucket != side).astype(jnp.int32)
    choice = is_outer + 2 * other_half
    return jnp.where(slot < counts_ref[half], choice, -1)


def product(query, key, features):
    return lax.dot_general(
        query, key, (((1,), (1,)), ((), ())), preferred_element_type=jnp.float32
    ) * (1.0 / math.sqrt(features))


def early_kernel(groups, lists_ref, counts_ref, mid_ref, outer_ref, mid2_ref, tiles_ref, unit_ref, out_sem):
    own_middle = lax.rem(lax.axis_index("feat"), ACROSS) == 1
    features = mid_ref.shape[1]
    keys = (mid_ref, outer_ref, mid2_ref)
    for value, query_ref in ((True, mid_ref), (False, outer_ref)):

        @pl.when(own_middle == value)
        def _(query_ref=query_ref):
            pltpu.make_async_copy(query_ref, unit_ref, out_sem).start()

    def fill(slot, carry):
        choice = listed(lists_ref, counts_ref, slot, groups)

        @pl.when((choice < 0) | (choice > 2))
        def _():
            tiles_ref[slot] = jnp.zeros(tiles_ref.shape[1:], jnp.float32)

        for value, query_ref in ((True, mid_ref), (False, outer_ref)):
            for index, key_ref in enumerate(keys):

                @pl.when((own_middle == value) & (choice == index))
                def _(query_ref=query_ref, key_ref=key_ref):
                    tiles_ref[slot] = product(query_ref[...], key_ref[...], features)

        return carry

    lax.fori_loop(0, tiles_ref.shape[0], fill, 0)
    pltpu.make_async_copy(mid_ref, unit_ref, out_sem).wait()


def late_kernel(groups, lists_ref, counts_ref, mid_ref, outer_ref, outer2_ref, early_ref, tiles_ref, tile, out_sem):
    own_middle = lax.rem(lax.axis_index("feat"), ACROSS) == 1
    features = mid_ref.shape[1]
    choices = [listed(lists_ref, counts_ref, slot, groups) for slot in range(early_ref.shape[0])]
    needed = functools.reduce(jnp.logical_or, [choice == 3 for choice in choices])
    slot = jnp.int32(0)
    for i, choice in enumerate(choices):
        slot = jnp.where(choice == 3, i, slot)
    for value, query_ref in ((True, mid_ref), (False, outer_ref)):

        @pl.when((own_middle == value) & needed)
        def _(query_ref=query_ref):
            tile[...] = product(query_ref[...], outer2_ref[...], features)

    @pl.when(needed)
    def _():
        out = pltpu.make_async_copy(tile, tiles_ref.at[slot], out_sem)
        out.start()
        out.wait()


def scores_early(lists, counts, mid, outer, mid2, groups):
    rows, features = mid.shape
    tiles = lists.shape[1]
    return pl.pallas_call(
        functools.partial(early_kernel, groups),
        in_specs=[SMEM, SMEM, VMEM, VMEM, VMEM],
        out_specs=[VMEM, HBM],
        out_shape=[
            jax.ShapeDtypeStruct((tiles, rows, rows), jnp.float32),
            jax.ShapeDtypeStruct((rows, features), jnp.bfloat16),
        ],
        scratch_shapes=[pltpu.SemaphoreType.DMA],
        compiler_params=pltpu.CompilerParams(vmem_limit_bytes=VMEM_LIMIT),
        cost_estimate=pl.CostEstimate(
            flops=4 * rows * rows * features, bytes_accessed=9 << 20, transcendentals=0
        ),
        name="early",
    )(lists, counts, mid, outer, mid2)


def scores_late(lists, counts, mid, outer, outer2, early, groups):
    rows, features = mid.shape
    return pl.pallas_call(
        functools.partial(late_kernel, groups),
        in_specs=[SMEM, SMEM, VMEM, VMEM, VMEM, HBM],
        out_specs=HBM,
        out_shape=jax.ShapeDtypeStruct(early.shape, early.dtype),
        scratch_shapes=[pltpu.VMEM((rows, rows), jnp.float32), pltpu.SemaphoreType.DMA],
        input_output_aliases={5: 0},
        compiler_params=pltpu.CompilerParams(vmem_limit_bytes=VMEM_LIMIT),
        cost_estimate=pl.CostEstimate(
            flops=2 * rows * rows * features, bytes_accessed=4 << 20, transcendentals=0
        ),
        name="late",
    )(lists, counts, mid, outer, outer2, early)


ORDER = (
    ("S2",),
    ("O3",),
    ("X0",),
    ("S1",),
    ("X1",),
    ("X2",),
    ("K1", "X0"),
    ("R2",),
    ("B3", "S2"),
    ("K2", "X1"),
    ("K3", "X1"),
    ("R3", "R2"),
    ("XO", "R2"),
    ("XB", "K1"),
)


OUTER = ("K0", "X0", "K1", "X1", "R3", "X2", "R2", "XO", "K2", "K3")
MIDDLE_AFTER = ("K2", "K3", "R3")


def after(value, *events):
    return lax.optimization_barrier((value, *events))[0]


def chip(at, side):
    return ACROSS * at + side


EVERY = tuple(range(ACROSS * ALONG))
DIRECT = (chip(0, 0), chip(1, 1), chip(2, 0), chip(3, 1))
RELAYED = (chip(1, 0), chip(0, 1), chip(3, 0), chip(2, 1))
NEAR = 1
FAR = (2, 3)


def hop_over(value, axis, mask, receivers=None):
    if receivers is None:
        receivers = range(lax.axis_size(axis))
    return lax.ppermute(value, axis, [(to ^ mask, to) for to in receivers])


def along(value, hop, receivers=EVERY):
    return hop_over(value, "feat", ACROSS * hop, receivers)


def across(value):
    return hop_over(value, "feat", 1)


def plain(index, pick=None):
    if pick is None:
        return lambda refs, place: refs[index][...]
    return lambda refs, place: refs[index][pick]


def kept_far(direct, relayed):
    def read(refs, place):
        straight = lax.rem(lax.div(place, ACROSS) + lax.rem(place, ACROSS), 2) == 0
        return jnp.where(straight, refs[direct][...], refs[relayed][...])

    return read


def paired(embeddings, signs, tile_blocks, tile_counts):
    groups = lax.axis_size("feat")
    width, columns = embeddings.shape
    rows = columns // groups
    table = jnp.asarray(parity_table(width), jnp.bfloat16)
    K0, S0, K1, S1, K2, S2, K3, B3, O3 = route(embeddings, signs, rows)
    plan = {
        "S1": lambda got: (S1, along, 1),
        "S2": lambda got: (S2, along, 2),
        "B3": lambda got: (B3, along, 3),
        "O3": lambda got: (O3, along, 3),
        "K1": lambda got: (K1, along, 1),
        "K2": lambda got: (K2, along, 2, DIRECT),
        "K3": lambda got: (K3, along, 3, DIRECT),
        "X0": lambda got: (S0, across),
        "X1": lambda got: (got["S1"], across),
        "X2": lambda got: (got["S2"], across),
        "XB": lambda got: (got["B3"], across),
        "XO": lambda got: (got["O3"], across),
        "R2": lambda got: (got["S2"][1], along, NEAR, RELAYED),
        "R3": lambda got: (got["O3"], along, NEAR, RELAYED),
    }
    got = {}
    for name, *events in ORDER:
        value, move, *rest = plan[name](got)
        if events:
            value = after(value, *(got[event] for event in events))
        with jax.named_scope(name):
            got[name] = move(value, *rest)
    first = S0
    if MIDDLE_AFTER:
        first = after(S0, *(got[name] for name in MIDDLE_AFTER))
    mid = rotate(
        [first, got["X0"], got["S1"], got["X1"], got["S2"], got["X2"], got["B3"], got["XB"]],
        [plain(i, 0 if i < 6 else None) for i in range(8)],
        table,
    )
    mid2 = hop_over(mid, "rows", 1)
    held = dict(got, K0=K0)
    at = {name: i for i, name in enumerate(OUTER)}
    outer = rotate(
        [held[name] for name in OUTER],
        [
            plain(at["K0"]),
            plain(at["X0"], 1),
            plain(at["K1"]),
            plain(at["X1"], 1),
            kept_far(at["K2"], at["R3"]),
            plain(at["X2"], 1),
            kept_far(at["K3"], at["R2"]),
            plain(at["XO"]),
        ],
        table,
    )
    outer2 = hop_over(outer, "rows", 1)
    lists = tile_blocks[:, 0, :]
    counts = tile_counts[:, 0]
    early, unit = scores_early(lists, counts, mid, outer, mid2, groups)
    tiles = scores_late(lists, counts, mid, outer, outer2, early, groups)
    return (tiles[None, None], unit[None])


def solution(mesh):
    body = paired if mesh.shape["feat"] == ALONG * ACROSS and mesh.shape["rows"] == 2 else general
    return jax.shard_map(
        body,
        mesh=mesh,
        in_specs=(
            P("feat", ("groups", "rows")),
            P("feat"),
            P("groups", "feat", None),
            P("groups", "feat"),
        ),
        out_specs=(
            P(("groups", "rows"), "feat", None, None, None),
            P(("groups", "rows"), "feat", None),
        ),
        check_vma=False,
    )
```

```python
import functools
import math

import jax
import jax.numpy as jnp
import numpy as np
from jax import lax
from jax.experimental import pallas as pl
from jax.experimental.pallas import tpu as pltpu
from jax.sharding import PartitionSpec as P

SMEM = pl.BlockSpec(memory_space=pltpu.SMEM)
VMEM = pl.BlockSpec(memory_space=pltpu.VMEM)
HBM = pl.BlockSpec(memory_space=pltpu.HBM)
VMEM_LIMIT = 24 << 20


def parity_table(length):
    positions = np.arange(length)
    shared = positions[:, None] & positions[None, :]
    parity = np.zeros_like(shared)
    while shared.any():
        parity ^= shared & 1
        shared = shared >> 1
    return 1 - 2 * parity


def from_partner(block, axis, distance):
    count = lax.axis_size(axis)
    route = []
    for low in range(count):
        high = low | 1 << distance
        if high != low and high < count:
            route += [(low, high), (high, low)]
    return lax.ppermute(block, axis, route)


def passed_along(value, axis, steps):
    count = lax.axis_size(axis)
    pairs = [(source, (source + steps) % count) for source in range(count)]
    return lax.ppermute(value, axis, pairs)


def general(embeddings, signs, tile_blocks, tile_counts):
    groups = lax.axis_size("feat")
    feat_place = lax.axis_index("feat")
    row_place = lax.axis_index("rows")
    signed = embeddings * signs.astype(jnp.bfloat16)[:, None]
    regrouped = lax.all_to_all(signed, "feat", split_axis=1, concat_axis=0, tiled=True)
    features = regrouped.shape[0]
    block_rows = regrouped.shape[1]
    local_width = features // groups
    score_scale = 1.0 / math.sqrt(features)
    inner_table = jnp.asarray(parity_table(local_width), jnp.bfloat16)
    outer_table = jnp.asarray(parity_table(groups), jnp.float32)
    blocked = regrouped.reshape(groups, local_width, block_rows)
    first_section = jnp.einsum(
        "abr,bc->acr", blocked, inner_table, preferred_element_type=jnp.float32
    )
    turned = (
        jnp.einsum("acr,ad->dcr", first_section, outer_table, precision=lax.Precision.HIGHEST)
        * score_scale
    )
    flattened = turned.reshape(features, block_rows)
    norm_factor = lax.rsqrt(jnp.mean(flattened * flattened, axis=0, keepdims=True) + 1e-06)
    unit_rows = (flattened * norm_factor).astype(jnp.bfloat16).T
    following = passed_along(unit_rows, "feat", -1)
    partner = from_partner(unit_rows, "rows", 0)
    following_partner = from_partner(following, "rows", 0)
    candidates = jnp.stack([unit_rows, following, partner, following_partner])
    tile_total = tile_blocks.shape[2]
    own_list = lax.dynamic_index_in_dim(tile_blocks[:, 0, :], row_place, 0, keepdims=False)
    own_count = lax.dynamic_index_in_dim(tile_counts[:, 0], row_place, 0, keepdims=False)

    def add_tile(slot_index, buffer):
        block_id = own_list[slot_index]
        other_half = (block_id // groups != row_place).astype(jnp.int32)
        other_bucket = (block_id % groups != feat_place).astype(jnp.int32)
        keyed_block = lax.dynamic_index_in_dim(
            candidates, other_bucket + 2 * other_half, 0, keepdims=False
        )
        tile_value = (
            lax.dot_general(
                unit_rows, keyed_block, (((1,), (1,)), ((), ())), preferred_element_type=jnp.float32
            )
            * score_scale
        )
        return lax.dynamic_update_index_in_dim(buffer, tile_value, slot_index, 0)

    empty_tiles = jnp.zeros((tile_total, block_rows, block_rows), jnp.float32)
    result = lax.fori_loop(0, own_count, add_tile, empty_tiles)
    return (result[None, None], unit_rows[None])


ACROSS = 2
ALONG = 4


def signs_kernel(signs_ref, wide_ref):
    step = signs_ref.shape[1]
    for i in range(signs_ref.shape[0]):
        tile = jnp.broadcast_to(signs_ref[i : i + 1, :].astype(jnp.float32), (step, step))
        tile = tile.T.astype(jnp.bfloat16)
        for low in range(0, wide_ref.shape[1], step):
            wide_ref[i * step : (i + 1) * step, low : low + step] = tile


def wanted(hop):
    place = lax.axis_index("feat")
    side = lax.rem(place, ACROSS)
    first = ACROSS * lax.bitwise_xor(lax.div(place, ACROSS), hop)
    last = lax.rem(first + ACROSS, ACROSS * ALONG)
    return jnp.where(side == 0, first, last), first + 1, jnp.where(side == 0, last, first)


def route_kernel(emb_ref, signs_ref, *refs):
    out_refs, (sign_rows, wide_ref, sign_sem, sems) = list(refs[:-4]), refs[-4:]
    sign_copy = pltpu.make_async_copy(signs_ref, sign_rows, sign_sem)
    sign_copy.start()
    targets = []
    for hop in range(ALONG):
        kept, middle, other = wanted(hop)
        targets.append((out_refs.pop(0), kept))
        if hop == ALONG - 1:
            targets += [(out_refs.pop(0), middle), (out_refs.pop(0), other)]
        else:
            shared = out_refs.pop(0)
            targets += [(shared.at[0], middle), (shared.at[1], other)]
    copies = []
    for i, (ref, block) in enumerate(targets):
        rows = ref.shape[1]
        start = pl.multiple_of(block * rows, rows)
        copies.append(pltpu.make_async_copy(emb_ref.at[:, pl.ds(start, rows)], ref, sems.at[i]))
    for copy in copies:
        copy.start()
    sign_copy.wait()
    signs_kernel(sign_rows, wide_ref)
    for copy, (ref, block) in zip(copies, targets):
        copy.wait()
        ref[...] = ref[...] * wide_ref[...]


def route(embeddings, signs, rows):
    width = embeddings.shape[0]
    one = jax.ShapeDtypeStruct((width, rows), jnp.bfloat16)
    two = jax.ShapeDtypeStruct((2, width, rows), jnp.bfloat16)
    out_shape = [one, two] * (ALONG - 1) + [one] * 3
    sign_rows = signs.reshape(width // 128, 128)
    return pl.pallas_call(
        route_kernel,
        in_specs=[HBM, HBM],
        out_specs=[VMEM] * len(out_shape),
        out_shape=out_shape,
        scratch_shapes=[
            pltpu.VMEM(sign_rows.shape, sign_rows.dtype),
            pltpu.VMEM((width, rows), jnp.bfloat16),
            pltpu.SemaphoreType.DMA,
            pltpu.SemaphoreType.DMA((3 * ALONG,)),
        ],
        compiler_params=pltpu.CompilerParams(vmem_limit_bytes=VMEM_LIMIT),
        cost_estimate=pl.CostEstimate(
            flops=3 * ALONG * width * rows,
            bytes_accessed=3 * ALONG * width * rows * 4,
            transcendentals=0,
        ),
        name="route",
    )(*(pltpu.with_memory_space_constraint(value, pltpu.HBM) for value in (embeddings, sign_rows)))


def butterfly(parts):
    parts = list(parts)
    half = 1
    while half < len(parts):
        for low in range(0, len(parts), 2 * half):
            for i in range(low, low + half):
                a, b = parts[i], parts[i + half]
                parts[i], parts[i + half] = a + b, a - b
        half *= 2
    return parts


def turned_parts(pieces, table_ref, low, chunk):
    return butterfly(
        lax.dot_general(
            piece,
            table_ref[:, low : low + chunk],
            (((0,), (0,)), ((), ())),
            preferred_element_type=jnp.float32,
        )
        for piece in pieces
    )


def begin_kernel(picks, *refs):
    table_ref, out_ref = refs[-2:]
    place = lax.axis_index("feat")
    pieces = [pick(refs, place) for pick in picks]
    width = pieces[0].shape[0]
    chunk = 256
    for low in range(0, width, chunk):
        for i, part in enumerate(turned_parts(pieces, table_ref, low, chunk)):
            out_ref[:, i * width + low : i * width + low + chunk] = part


def begin(inputs, picks, table):
    count = len(picks)
    width, rows = inputs[0].shape[-2:]
    return pl.pallas_call(
        functools.partial(begin_kernel, picks),
        in_specs=[VMEM] * (len(inputs) + 1),
        out_specs=VMEM,
        out_shape=jax.ShapeDtypeStruct((rows, count * width), jnp.float32),
        compiler_params=pltpu.CompilerParams(vmem_limit_bytes=VMEM_LIMIT),
        cost_estimate=pl.CostEstimate(
            flops=2 * rows * count * width * width, bytes_accessed=3 << 20, transcendentals=0
        ),
        name="begin",
    )(*inputs, table)


def finish_kernel(picks, *refs):
    begun_ref, table_ref, out_ref, turned = refs[-4:]
    place = lax.axis_index("feat")
    pieces = [pick(refs, place) for pick in picks]
    width, rows = pieces[0].shape
    half = len(pieces)
    count = 2 * half
    features = count * width
    chunk = 256
    total = jnp.zeros((rows, 128), jnp.float32)
    for low in range(0, width, chunk):
        for i, late in enumerate(turned_parts(pieces, table_ref, low, chunk)):
            early = begun_ref[:, i * width + low : i * width + low + chunk]
            for place_out, part in ((i, early + late), (i + half, early - late)):
                turned[:, place_out * width + low : place_out * width + low + chunk] = part
                square = part * part
                for lane in range(0, chunk, 128):
                    total = total + square[:, lane : lane + 128]
    mean = jnp.sum(total, axis=1, keepdims=True) * (1.0 / (features * features))
    factor = lax.rsqrt(mean + 1e-06) * (1.0 / math.sqrt(features))
    for i in range(count):
        odd = jnp.int32(0)
        for bit in range(count.bit_length() - 1):
            if i >> bit & 1:
                odd = odd + (lax.shift_right_logical(place, bit) & 1)
        sign = (1 - 2 * (odd & 1)).astype(jnp.float32)
        columns = slice(i * width, (i + 1) * width)
        out_ref[:, columns] = (turned[:, columns] * (factor * sign)).astype(jnp.bfloat16)


def finish(inputs, picks, begun, table):
    count = 2 * len(picks)
    width, rows = inputs[0].shape[-2:]
    return pl.pallas_call(
        functools.partial(finish_kernel, picks),
        in_specs=[VMEM] * (len(inputs) + 2),
        out_specs=VMEM,
        out_shape=jax.ShapeDtypeStruct((rows, count * width), jnp.bfloat16),
        scratch_shapes=[pltpu.VMEM((rows, count * width), jnp.float32)],
        compiler_params=pltpu.CompilerParams(vmem_limit_bytes=VMEM_LIMIT),
        cost_estimate=pl.CostEstimate(
            flops=rows * count * width * width, bytes_accessed=5 << 20, transcendentals=0
        ),
        name="finish",
    )(*inputs, begun, table)


def listed(lists_ref, counts_ref, slot, groups):
    place = lax.axis_index("feat")
    half = lax.axis_index("rows")
    block_id = lists_ref[half, slot]
    other_half = (lax.div(block_id, groups) != half).astype(jnp.int32)
    own_bucket = (lax.rem(block_id, groups) == place).astype(jnp.int32)
    side = lax.rem(place, ACROSS)
    is_outer = (own_bucket != side).astype(jnp.int32)
    choice = is_outer + 2 * other_half
    return jnp.where(slot < counts_ref[half], choice, -1)


def product(query, key, features):
    return lax.dot_general(
        query, key, (((1,), (1,)), ((), ())), preferred_element_type=jnp.float32
    ) * (1.0 / math.sqrt(features))


def early_kernel(groups, lists_ref, counts_ref, mid_ref, outer_ref, mid2_ref, tiles_ref, unit_ref, out_sem):
    own_middle = lax.rem(lax.axis_index("feat"), ACROSS) == 1
    features = mid_ref.shape[1]
    keys = (mid_ref, outer_ref, mid2_ref)
    for value, query_ref in ((True, mid_ref), (False, outer_ref)):

        @pl.when(own_middle == value)
        def _(query_ref=query_ref):
            pltpu.make_async_copy(query_ref, unit_ref, out_sem).start()

    def fill(slot, carry):
        choice = listed(lists_ref, counts_ref, slot, groups)

        @pl.when((choice < 0) | (choice > 2))
        def _():
            tiles_ref[slot] = jnp.zeros(tiles_ref.shape[1:], jnp.float32)

        for value, query_ref in ((True, mid_ref), (False, outer_ref)):
            for index, key_ref in enumerate(keys):

                @pl.when((own_middle == value) & (choice == index))
                def _(query_ref=query_ref, key_ref=key_ref):
                    tiles_ref[slot] = product(query_ref[...], key_ref[...], features)

        return carry

    lax.fori_loop(0, tiles_ref.shape[0], fill, 0)
    pltpu.make_async_copy(mid_ref, unit_ref, out_sem).wait()


def late_kernel(groups, lists_ref, counts_ref, mid_ref, outer_ref, outer2_ref, early_ref, tiles_ref, tile, out_sem):
    own_middle = lax.rem(lax.axis_index("feat"), ACROSS) == 1
    features = mid_ref.shape[1]
    choices = [listed(lists_ref, counts_ref, slot, groups) for slot in range(early_ref.shape[0])]
    needed = functools.reduce(jnp.logical_or, [choice == 3 for choice in choices])
    slot = jnp.int32(0)
    for i, choice in enumerate(choices):
        slot = jnp.where(choice == 3, i, slot)
    for value, query_ref in ((True, mid_ref), (False, outer_ref)):

        @pl.when((own_middle == value) & needed)
        def _(query_ref=query_ref):
            tile[...] = product(query_ref[...], outer2_ref[...], features)

    @pl.when(needed)
    def _():
        out = pltpu.make_async_copy(tile, tiles_ref.at[slot], out_sem)
        out.start()
        out.wait()


def scores_early(lists, counts, mid, outer, mid2, groups):
    rows, features = mid.shape
    tiles = lists.shape[1]
    return pl.pallas_call(
        functools.partial(early_kernel, groups),
        in_specs=[SMEM, SMEM, VMEM, VMEM, VMEM],
        out_specs=[VMEM, HBM],
        out_shape=[
            jax.ShapeDtypeStruct((tiles, rows, rows), jnp.float32),
            jax.ShapeDtypeStruct((rows, features), jnp.bfloat16),
        ],
        scratch_shapes=[pltpu.SemaphoreType.DMA],
        compiler_params=pltpu.CompilerParams(vmem_limit_bytes=VMEM_LIMIT),
        cost_estimate=pl.CostEstimate(
            flops=4 * rows * rows * features, bytes_accessed=9 << 20, transcendentals=0
        ),
        name="early",
    )(lists, counts, mid, outer, mid2)


def scores_late(lists, counts, mid, outer, outer2, early, groups):
    rows, features = mid.shape
    return pl.pallas_call(
        functools.partial(late_kernel, groups),
        in_specs=[SMEM, SMEM, VMEM, VMEM, VMEM, HBM],
        out_specs=HBM,
        out_shape=jax.ShapeDtypeStruct(early.shape, early.dtype),
        scratch_shapes=[pltpu.VMEM((rows, rows), jnp.float32), pltpu.SemaphoreType.DMA],
        input_output_aliases={5: 0},
        compiler_params=pltpu.CompilerParams(vmem_limit_bytes=VMEM_LIMIT),
        cost_estimate=pl.CostEstimate(
            flops=2 * rows * rows * features, bytes_accessed=4 << 20, transcendentals=0
        ),
        name="late",
    )(lists, counts, mid, outer, outer2, early)


ORDER = (
    ("S2",),
    ("O3",),
    ("X0",),
    ("S1",),
    ("X1",),
    ("X2",),
    ("K1", "X0"),
    ("R2",),
    ("B3", "S2"),
    ("K2", "X1"),
    ("K3", "X1"),
    ("R3", "R2"),
    ("XO", "R2"),
    ("XB", "K1"),
)


MIDDLE_AFTER = ("K2", "K3", "R3")


def after(value, *events):
    return lax.optimization_barrier((value, *events))[0]


def chip(at, side):
    return ACROSS * at + side


EVERY = tuple(range(ACROSS * ALONG))
DIRECT = (chip(0, 0), chip(1, 1), chip(2, 0), chip(3, 1))
RELAYED = (chip(1, 0), chip(0, 1), chip(3, 0), chip(2, 1))
NEAR = 1
FAR = (2, 3)


def hop_over(value, axis, mask, receivers=None):
    if receivers is None:
        receivers = range(lax.axis_size(axis))
    return lax.ppermute(value, axis, [(to ^ mask, to) for to in receivers])


def along(value, hop, receivers=EVERY):
    return hop_over(value, "feat", ACROSS * hop, receivers)


def across(value):
    return hop_over(value, "feat", 1)


def plain(index, pick=None):
    if pick is None:
        return lambda refs, place: refs[index][...]
    return lambda refs, place: refs[index][pick]


def kept_far(direct, relayed):
    def read(refs, place):
        straight = lax.rem(lax.div(place, ACROSS) + lax.rem(place, ACROSS), 2) == 0
        return jnp.where(straight, refs[direct][...], refs[relayed][...])

    return read


def paired(embeddings, signs, tile_blocks, tile_counts):
    groups = lax.axis_size("feat")
    width, columns = embeddings.shape
    rows = columns // groups
    table = jnp.asarray(parity_table(width), jnp.bfloat16)
    K0, S0, K1, S1, K2, S2, K3, B3, O3 = route(embeddings, signs, rows)
    plan = {
        "S1": lambda got: (S1, along, 1),
        "S2": lambda got: (S2, along, 2),
        "B3": lambda got: (B3, along, 3),
        "O3": lambda got: (O3, along, 3),
        "K1": lambda got: (K1, along, 1),
        "K2": lambda got: (K2, along, 2, DIRECT),
        "K3": lambda got: (K3, along, 3, DIRECT),
        "X0": lambda got: (S0, across),
        "X1": lambda got: (got["S1"], across),
        "X2": lambda got: (got["S2"], across),
        "XB": lambda got: (got["B3"], across),
        "XO": lambda got: (got["O3"], across),
        "R2": lambda got: (got["S2"][1], along, NEAR, RELAYED),
        "R3": lambda got: (got["O3"], along, NEAR, RELAYED),
    }
    got = {}
    for name, *events in ORDER:
        value, move, *rest = plan[name](got)
        if events:
            value = after(value, *(got[event] for event in events))
        with jax.named_scope(name):
            got[name] = move(value, *rest)
    mid_begun = begin(
        [S0, got["X0"], got["S1"], got["X1"]], [plain(i, 0) for i in range(4)], table
    )
    outer_begun = begin(
        [K0, got["X0"], got["K1"], got["X1"]],
        [plain(0), plain(1, 1), plain(2), plain(3, 1)],
        table,
    )
    first = after(got["S2"], *(got[name] for name in MIDDLE_AFTER))
    mid = finish(
        [first, got["X2"], got["B3"], got["XB"]],
        [plain(0, 0), plain(1, 0), plain(2), plain(3)],
        mid_begun,
        table,
    )
    mid2 = hop_over(mid, "rows", 1)
    outer = finish(
        [got["K2"], got["R3"], got["X2"], got["K3"], got["R2"], got["XO"]],
        [kept_far(0, 1), plain(2, 1), kept_far(3, 4), plain(5)],
        outer_begun,
        table,
    )
    outer2 = hop_over(outer, "rows", 1)
    lists = tile_blocks[:, 0, :]
    counts = tile_counts[:, 0]
    early, unit = scores_early(lists, counts, mid, outer, mid2, groups)
    tiles = scores_late(lists, counts, mid, outer, outer2, early, groups)
    return (tiles[None, None], unit[None])


def solution(mesh):
    body = paired if mesh.shape["feat"] == ALONG * ACROSS and mesh.shape["rows"] == 2 else general
    return jax.shard_map(
        body,
        mesh=mesh,
        in_specs=(
            P("feat", ("groups", "rows")),
            P("feat"),
            P("groups", "feat", None),
            P("groups", "feat"),
        ),
        out_specs=(
            P(("groups", "rows"), "feat", None, None, None),
            P(("groups", "rows"), "feat", None),
        ),
        check_vma=False,
    )
```

```python
import functools
import math

import jax
import jax.numpy as jnp
import numpy as np
from jax import lax
from jax.experimental import pallas as pl
from jax.experimental.pallas import tpu as pltpu
from jax.sharding import PartitionSpec as P

SMEM = pl.BlockSpec(memory_space=pltpu.SMEM)
VMEM = pl.BlockSpec(memory_space=pltpu.VMEM)
HBM = pl.BlockSpec(memory_space=pltpu.HBM)
VMEM_LIMIT = 24 << 20


def parity_table(length):
    positions = np.arange(length)
    shared = positions[:, None] & positions[None, :]
    parity = np.zeros_like(shared)
    while shared.any():
        parity ^= shared & 1
        shared = shared >> 1
    return 1 - 2 * parity


def from_partner(block, axis, distance):
    count = lax.axis_size(axis)
    route = []
    for low in range(count):
        high = low | 1 << distance
        if high != low and high < count:
            route += [(low, high), (high, low)]
    return lax.ppermute(block, axis, route)


def passed_along(value, axis, steps):
    count = lax.axis_size(axis)
    pairs = [(source, (source + steps) % count) for source in range(count)]
    return lax.ppermute(value, axis, pairs)


def general(embeddings, signs, tile_blocks, tile_counts):
    groups = lax.axis_size("feat")
    feat_place = lax.axis_index("feat")
    row_place = lax.axis_index("rows")
    signed = embeddings * signs.astype(jnp.bfloat16)[:, None]
    regrouped = lax.all_to_all(signed, "feat", split_axis=1, concat_axis=0, tiled=True)
    features = regrouped.shape[0]
    block_rows = regrouped.shape[1]
    local_width = features // groups
    score_scale = 1.0 / math.sqrt(features)
    inner_table = jnp.asarray(parity_table(local_width), jnp.bfloat16)
    outer_table = jnp.asarray(parity_table(groups), jnp.float32)
    blocked = regrouped.reshape(groups, local_width, block_rows)
    first_section = jnp.einsum(
        "abr,bc->acr", blocked, inner_table, preferred_element_type=jnp.float32
    )
    turned = (
        jnp.einsum("acr,ad->dcr", first_section, outer_table, precision=lax.Precision.HIGHEST)
        * score_scale
    )
    flattened = turned.reshape(features, block_rows)
    norm_factor = lax.rsqrt(jnp.mean(flattened * flattened, axis=0, keepdims=True) + 1e-06)
    unit_rows = (flattened * norm_factor).astype(jnp.bfloat16).T
    following = passed_along(unit_rows, "feat", -1)
    partner = from_partner(unit_rows, "rows", 0)
    following_partner = from_partner(following, "rows", 0)
    candidates = jnp.stack([unit_rows, following, partner, following_partner])
    tile_total = tile_blocks.shape[2]
    own_list = lax.dynamic_index_in_dim(tile_blocks[:, 0, :], row_place, 0, keepdims=False)
    own_count = lax.dynamic_index_in_dim(tile_counts[:, 0], row_place, 0, keepdims=False)

    def add_tile(slot_index, buffer):
        block_id = own_list[slot_index]
        other_half = (block_id // groups != row_place).astype(jnp.int32)
        other_bucket = (block_id % groups != feat_place).astype(jnp.int32)
        keyed_block = lax.dynamic_index_in_dim(
            candidates, other_bucket + 2 * other_half, 0, keepdims=False
        )
        tile_value = (
            lax.dot_general(
                unit_rows, keyed_block, (((1,), (1,)), ((), ())), preferred_element_type=jnp.float32
            )
            * score_scale
        )
        return lax.dynamic_update_index_in_dim(buffer, tile_value, slot_index, 0)

    empty_tiles = jnp.zeros((tile_total, block_rows, block_rows), jnp.float32)
    result = lax.fori_loop(0, own_count, add_tile, empty_tiles)
    return (result[None, None], unit_rows[None])


ACROSS = 2
ALONG = 4


def signs_kernel(signs_ref, wide_ref):
    step = signs_ref.shape[1]
    for i in range(signs_ref.shape[0]):
        tile = jnp.broadcast_to(signs_ref[i : i + 1, :].astype(jnp.float32), (step, step))
        tile = tile.T.astype(jnp.bfloat16)
        for low in range(0, wide_ref.shape[1], step):
            wide_ref[i * step : (i + 1) * step, low : low + step] = tile


def wanted(hop):
    place = lax.axis_index("feat")
    side = lax.rem(place, ACROSS)
    first = ACROSS * lax.bitwise_xor(lax.div(place, ACROSS), hop)
    last = lax.rem(first + ACROSS, ACROSS * ALONG)
    return jnp.where(side == 0, first, last), first + 1, jnp.where(side == 0, last, first)


KEPT, MIDDLE, OTHER = range(3)
ROUTED_FIRST = (((0, MIDDLE), (0, OTHER)), ((1, MIDDLE), (1, OTHER)), ((2, MIDDLE), (2, OTHER)), ((3, OTHER),))
ROUTED_LATER = (((0, KEPT),), ((1, KEPT),), ((2, KEPT),), ((3, KEPT),), ((3, MIDDLE),))


def route_kernel(groups, emb_ref, *refs):
    first_call = groups is ROUTED_FIRST
    signs_ref, refs = refs[0], list(refs[1:])
    if first_call:
        sign_sem, sign_rows = refs.pop(), refs.pop()
        sign_copy = pltpu.make_async_copy(signs_ref, sign_rows, sign_sem)
        sign_copy.start()
    sems = refs.pop()
    wide_ref = refs.pop() if first_call else signs_ref
    targets = []
    for ref, blocks in zip(refs, groups):
        for i, (hop, kind) in enumerate(blocks):
            targets.append((ref.at[i] if len(blocks) > 1 else ref, wanted(hop)[kind]))
    copies = []
    for i, (ref, block) in enumerate(targets):
        rows = ref.shape[1]
        start = pl.multiple_of(block * rows, rows)
        copies.append(pltpu.make_async_copy(emb_ref.at[:, pl.ds(start, rows)], ref, sems.at[i]))
    for copy in copies:
        copy.start()
    if first_call:
        sign_copy.wait()
        signs_kernel(sign_rows, wide_ref)
    for copy, (ref, block) in zip(copies, targets):
        copy.wait()
        ref[...] = ref[...] * wide_ref[...]


def route(embeddings, signs, rows, groups):
    width = embeddings.shape[0]
    first_call = groups is ROUTED_FIRST
    shapes = [(width, rows) if len(blocks) == 1 else (len(blocks), width, rows) for blocks in groups]
    count = sum(len(blocks) for blocks in groups)
    scratch = [pltpu.SemaphoreType.DMA((count,))]
    if first_call:
        shapes.append((width, rows))
        signs = signs.reshape(width // 128, 128)
        scratch += [pltpu.VMEM(signs.shape, signs.dtype), pltpu.SemaphoreType.DMA]
        signs = pltpu.with_memory_space_constraint(signs, pltpu.HBM)
    return pl.pallas_call(
        functools.partial(route_kernel, groups),
        in_specs=[HBM, HBM if first_call else VMEM],
        out_specs=[VMEM] * len(shapes),
        out_shape=[jax.ShapeDtypeStruct(shape, jnp.bfloat16) for shape in shapes],
        scratch_shapes=scratch,
        compiler_params=pltpu.CompilerParams(vmem_limit_bytes=VMEM_LIMIT),
        cost_estimate=pl.CostEstimate(
            flops=count * width * rows, bytes_accessed=count * width * rows * 4, transcendentals=0
        ),
        name="route",
    )(pltpu.with_memory_space_constraint(embeddings, pltpu.HBM), signs)


def butterfly(parts):
    parts = list(parts)
    half = 1
    while half < len(parts):
        for low in range(0, len(parts), 2 * half):
            for i in range(low, low + half):
                a, b = parts[i], parts[i + half]
                parts[i], parts[i + half] = a + b, a - b
        half *= 2
    return parts


def turned_parts(pieces, table_ref, low, chunk):
    return butterfly(
        lax.dot_general(
            piece,
            table_ref[:, low : low + chunk],
            (((0,), (0,)), ((), ())),
            preferred_element_type=jnp.float32,
        )
        for piece in pieces
    )


def begin_kernel(picks, *refs):
    table_ref, out_ref = refs[-2:]
    place = lax.axis_index("feat")
    pieces = [pick(refs, place) for pick in picks]
    width = pieces[0].shape[0]
    chunk = 256
    for low in range(0, width, chunk):
        for i, part in enumerate(turned_parts(pieces, table_ref, low, chunk)):
            out_ref[:, i * width + low : i * width + low + chunk] = part


def begin(inputs, picks, table):
    count = len(picks)
    width, rows = inputs[0].shape[-2:]
    return pl.pallas_call(
        functools.partial(begin_kernel, picks),
        in_specs=[VMEM] * (len(inputs) + 1),
        out_specs=VMEM,
        out_shape=jax.ShapeDtypeStruct((rows, count * width), jnp.float32),
        compiler_params=pltpu.CompilerParams(vmem_limit_bytes=VMEM_LIMIT),
        cost_estimate=pl.CostEstimate(
            flops=2 * rows * count * width * width, bytes_accessed=3 << 20, transcendentals=0
        ),
        name="begin",
    )(*inputs, table)


def finish_kernel(picks, *refs):
    begun_ref, table_ref, out_ref, turned = refs[-4:]
    place = lax.axis_index("feat")
    pieces = [pick(refs, place) for pick in picks]
    width, rows = pieces[0].shape
    half = len(pieces)
    count = 2 * half
    features = count * width
    chunk = 256
    total = jnp.zeros((rows, 128), jnp.float32)
    for low in range(0, width, chunk):
        for i, late in enumerate(turned_parts(pieces, table_ref, low, chunk)):
            early = begun_ref[:, i * width + low : i * width + low + chunk]
            for place_out, part in ((i, early + late), (i + half, early - late)):
                turned[:, place_out * width + low : place_out * width + low + chunk] = part
                square = part * part
                for lane in range(0, chunk, 128):
                    total = total + square[:, lane : lane + 128]
    mean = jnp.sum(total, axis=1, keepdims=True) * (1.0 / (features * features))
    factor = lax.rsqrt(mean + 1e-06) * (1.0 / math.sqrt(features))
    for i in range(count):
        odd = jnp.int32(0)
        for bit in range(count.bit_length() - 1):
            if i >> bit & 1:
                odd = odd + (lax.shift_right_logical(place, bit) & 1)
        sign = (1 - 2 * (odd & 1)).astype(jnp.float32)
        columns = slice(i * width, (i + 1) * width)
        out_ref[:, columns] = (turned[:, columns] * (factor * sign)).astype(jnp.bfloat16)


def finish(inputs, picks, begun, table):
    count = 2 * len(picks)
    width, rows = inputs[0].shape[-2:]
    return pl.pallas_call(
        functools.partial(finish_kernel, picks),
        in_specs=[VMEM] * (len(inputs) + 2),
        out_specs=VMEM,
        out_shape=jax.ShapeDtypeStruct((rows, count * width), jnp.bfloat16),
        scratch_shapes=[pltpu.VMEM((rows, count * width), jnp.float32)],
        compiler_params=pltpu.CompilerParams(vmem_limit_bytes=VMEM_LIMIT),
        cost_estimate=pl.CostEstimate(
            flops=rows * count * width * width, bytes_accessed=5 << 20, transcendentals=0
        ),
        name="finish",
    )(*inputs, begun, table)


def listed(lists_ref, counts_ref, slot, groups):
    place = lax.axis_index("feat")
    half = lax.axis_index("rows")
    block_id = lists_ref[half, slot]
    other_half = (lax.div(block_id, groups) != half).astype(jnp.int32)
    own_bucket = (lax.rem(block_id, groups) == place).astype(jnp.int32)
    side = lax.rem(place, ACROSS)
    is_outer = (own_bucket != side).astype(jnp.int32)
    choice = is_outer + 2 * other_half
    return jnp.where(slot < counts_ref[half], choice, -1)


def product(query, key, features):
    return lax.dot_general(
        query, key, (((1,), (1,)), ((), ())), preferred_element_type=jnp.float32
    ) * (1.0 / math.sqrt(features))


def early_kernel(groups, lists_ref, counts_ref, mid_ref, outer_ref, mid2_ref, tiles_ref, unit_ref, out_sem):
    own_middle = lax.rem(lax.axis_index("feat"), ACROSS) == 1
    features = mid_ref.shape[1]
    keys = (mid_ref, outer_ref, mid2_ref)
    for value, query_ref in ((True, mid_ref), (False, outer_ref)):

        @pl.when(own_middle == value)
        def _(query_ref=query_ref):
            pltpu.make_async_copy(query_ref, unit_ref, out_sem).start()

    def fill(slot, carry):
        choice = listed(lists_ref, counts_ref, slot, groups)

        @pl.when((choice < 0) | (choice > 2))
        def _():
            tiles_ref[slot] = jnp.zeros(tiles_ref.shape[1:], jnp.float32)

        for value, query_ref in ((True, mid_ref), (False, outer_ref)):
            for index, key_ref in enumerate(keys):

                @pl.when((own_middle == value) & (choice == index))
                def _(query_ref=query_ref, key_ref=key_ref):
                    tiles_ref[slot] = product(query_ref[...], key_ref[...], features)

        return carry

    lax.fori_loop(0, tiles_ref.shape[0], fill, 0)
    pltpu.make_async_copy(mid_ref, unit_ref, out_sem).wait()


def late_kernel(groups, lists_ref, counts_ref, mid_ref, outer_ref, outer2_ref, early_ref, tiles_ref, tile, out_sem):
    own_middle = lax.rem(lax.axis_index("feat"), ACROSS) == 1
    features = mid_ref.shape[1]
    choices = [listed(lists_ref, counts_ref, slot, groups) for slot in range(early_ref.shape[0])]
    needed = functools.reduce(jnp.logical_or, [choice == 3 for choice in choices])
    slot = jnp.int32(0)
    for i, choice in enumerate(choices):
        slot = jnp.where(choice == 3, i, slot)
    for value, query_ref in ((True, mid_ref), (False, outer_ref)):

        @pl.when((own_middle == value) & needed)
        def _(query_ref=query_ref):
            tile[...] = product(query_ref[...], outer2_ref[...], features)

    @pl.when(needed)
    def _():
        out = pltpu.make_async_copy(tile, tiles_ref.at[slot], out_sem)
        out.start()
        out.wait()


def scores_early(lists, counts, mid, outer, mid2, groups):
    rows, features = mid.shape
    tiles = lists.shape[1]
    return pl.pallas_call(
        functools.partial(early_kernel, groups),
        in_specs=[SMEM, SMEM, VMEM, VMEM, VMEM],
        out_specs=[VMEM, HBM],
        out_shape=[
            jax.ShapeDtypeStruct((tiles, rows, rows), jnp.float32),
            jax.ShapeDtypeStruct((rows, features), jnp.bfloat16),
        ],
        scratch_shapes=[pltpu.SemaphoreType.DMA],
        compiler_params=pltpu.CompilerParams(vmem_limit_bytes=VMEM_LIMIT),
        cost_estimate=pl.CostEstimate(
            flops=4 * rows * rows * features, bytes_accessed=9 << 20, transcendentals=0
        ),
        name="early",
    )(lists, counts, mid, outer, mid2)


def scores_late(lists, counts, mid, outer, outer2, early, groups):
    rows, features = mid.shape
    return pl.pallas_call(
        functools.partial(late_kernel, groups),
        in_specs=[SMEM, SMEM, VMEM, VMEM, VMEM, HBM],
        out_specs=HBM,
        out_shape=jax.ShapeDtypeStruct(early.shape, early.dtype),
        scratch_shapes=[pltpu.VMEM((rows, rows), jnp.float32), pltpu.SemaphoreType.DMA],
        input_output_aliases={5: 0},
        compiler_params=pltpu.CompilerParams(vmem_limit_bytes=VMEM_LIMIT),
        cost_estimate=pl.CostEstimate(
            flops=2 * rows * rows * features, bytes_accessed=4 << 20, transcendentals=0
        ),
        name="late",
    )(lists, counts, mid, outer, outer2, early)


ORDER = (
    ("S2",),
    ("O3",),
    ("X0",),
    ("S1",),
    ("X1",),
    ("X2",),
    ("K1", "X0"),
    ("R2", "K0"),
    ("B3", "S2"),
    ("K2", "X1"),
    ("R3", "R2"),
    ("XO", "R2"),
    ("XB", "K1"),
    ("K3", "B3"),
)


ROUTE_AFTER = "S1"
MIDDLE_AFTER = ("K2", "R3")


def after(value, *events):
    return lax.optimization_barrier((value, *events))[0]


def chip(at, side):
    return ACROSS * at + side


EVERY = tuple(range(ACROSS * ALONG))
DIRECT = (chip(0, 0), chip(1, 1), chip(2, 0), chip(3, 1))
RELAYED = (chip(1, 0), chip(0, 1), chip(3, 0), chip(2, 1))
NEAR = 1
FAR = (2, 3)


def hop_over(value, axis, mask, receivers=None):
    if receivers is None:
        receivers = range(lax.axis_size(axis))
    return lax.ppermute(value, axis, [(to ^ mask, to) for to in receivers])


def along(value, hop, receivers=EVERY):
    return hop_over(value, "feat", ACROSS * hop, receivers)


def across(value):
    return hop_over(value, "feat", 1)


def plain(index, pick=None):
    if pick is None:
        return lambda refs, place: refs[index][...]
    return lambda refs, place: refs[index][pick]


def kept_far(direct, relayed):
    def read(refs, place):
        straight = lax.rem(lax.div(place, ACROSS) + lax.rem(place, ACROSS), 2) == 0
        return jnp.where(straight, refs[direct][...], refs[relayed][...])

    return read


def paired(embeddings, signs, tile_blocks, tile_counts):
    groups = lax.axis_size("feat")
    width, columns = embeddings.shape
    rows = columns // groups
    table = jnp.asarray(parity_table(width), jnp.bfloat16)
    S0, S1, S2, O3, wide = route(embeddings, signs, rows, ROUTED_FIRST)
    late = {}
    plan = {
        "S1": lambda got: (S1, along, 1),
        "S2": lambda got: (S2, along, 2),
        "B3": lambda got: (late["B3"], along, 3),
        "O3": lambda got: (O3, along, 3),
        "K1": lambda got: (late["K1"], along, 1),
        "K2": lambda got: (late["K2"], along, 2, DIRECT),
        "K3": lambda got: (late["K3"], along, 3, DIRECT),
        "X0": lambda got: (S0, across),
        "X1": lambda got: (got["S1"], across),
        "X2": lambda got: (got["S2"], across),
        "XB": lambda got: (got["B3"], across),
        "XO": lambda got: (got["O3"], across),
        "R2": lambda got: (got["S2"][1], along, NEAR, RELAYED),
        "R3": lambda got: (got["O3"], along, NEAR, RELAYED),
    }
    got = {}
    for name, *events in ORDER:
        if not late and ROUTE_AFTER in got:
            rest = route(embeddings, after(wide, got[ROUTE_AFTER]), rows, ROUTED_LATER)
            late = dict(zip(("K0", "K1", "K2", "K3", "B3"), rest))
        value, move, *rest = plan[name](got)
        if events:
            value = after(value, *(got.get(event, late.get(event)) for event in events))
        with jax.named_scope(name):
            got[name] = move(value, *rest)
    mid_begun = begin(
        [S0, got["X0"], got["S1"], got["X1"]], [plain(i, 0) for i in range(4)], table
    )
    outer_begun = begin(
        [late["K0"], got["X0"], got["K1"], got["X1"]],
        [plain(0), plain(1, 1), plain(2), plain(3, 1)],
        table,
    )
    first = after(got["S2"], *(got[name] for name in MIDDLE_AFTER))
    mid = finish(
        [first, got["X2"], got["B3"], got["XB"]],
        [plain(0, 0), plain(1, 0), plain(2), plain(3)],
        mid_begun,
        table,
    )
    mid2 = hop_over(mid, "rows", 1)
    outer = finish(
        [got["K2"], got["R3"], got["X2"], got["K3"], got["R2"], got["XO"]],
        [kept_far(0, 1), plain(2, 1), kept_far(3, 4), plain(5)],
        outer_begun,
        table,
    )
    outer2 = hop_over(outer, "rows", 1)
    lists = tile_blocks[:, 0, :]
    counts = tile_counts[:, 0]
    early, unit = scores_early(lists, counts, mid, outer, mid2, groups)
    tiles = scores_late(lists, counts, mid, outer, outer2, early, groups)
    return (tiles[None, None], unit[None])


def solution(mesh):
    body = paired if mesh.shape["feat"] == ALONG * ACROSS and mesh.shape["rows"] == 2 else general
    return jax.shard_map(
        body,
        mesh=mesh,
        in_specs=(
            P("feat", ("groups", "rows")),
            P("feat"),
            P("groups", "feat", None),
            P("groups", "feat"),
        ),
        out_specs=(
            P(("groups", "rows"), "feat", None, None, None),
            P(("groups", "rows"), "feat", None),
        ),
        check_vma=False,
    )
```

```python
import functools
import math

import jax
import jax.numpy as jnp
import numpy as np
from jax import lax
from jax.experimental import pallas as pl
from jax.experimental.pallas import tpu as pltpu
from jax.sharding import PartitionSpec as P

SMEM = pl.BlockSpec(memory_space=pltpu.SMEM)
VMEM = pl.BlockSpec(memory_space=pltpu.VMEM)
HBM = pl.BlockSpec(memory_space=pltpu.HBM)
VMEM_LIMIT = 24 << 20


def parity_table(length):
    positions = np.arange(length)
    shared = positions[:, None] & positions[None, :]
    parity = np.zeros_like(shared)
    while shared.any():
        parity ^= shared & 1
        shared = shared >> 1
    return 1 - 2 * parity


def from_partner(block, axis, distance):
    count = lax.axis_size(axis)
    route = []
    for low in range(count):
        high = low | 1 << distance
        if high != low and high < count:
            route += [(low, high), (high, low)]
    return lax.ppermute(block, axis, route)


def passed_along(value, axis, steps):
    count = lax.axis_size(axis)
    pairs = [(source, (source + steps) % count) for source in range(count)]
    return lax.ppermute(value, axis, pairs)


def general(embeddings, signs, tile_blocks, tile_counts):
    groups = lax.axis_size("feat")
    feat_place = lax.axis_index("feat")
    row_place = lax.axis_index("rows")
    signed = embeddings * signs.astype(jnp.bfloat16)[:, None]
    regrouped = lax.all_to_all(signed, "feat", split_axis=1, concat_axis=0, tiled=True)
    features = regrouped.shape[0]
    block_rows = regrouped.shape[1]
    local_width = features // groups
    score_scale = 1.0 / math.sqrt(features)
    inner_table = jnp.asarray(parity_table(local_width), jnp.bfloat16)
    outer_table = jnp.asarray(parity_table(groups), jnp.float32)
    blocked = regrouped.reshape(groups, local_width, block_rows)
    first_section = jnp.einsum(
        "abr,bc->acr", blocked, inner_table, preferred_element_type=jnp.float32
    )
    turned = (
        jnp.einsum("acr,ad->dcr", first_section, outer_table, precision=lax.Precision.HIGHEST)
        * score_scale
    )
    flattened = turned.reshape(features, block_rows)
    norm_factor = lax.rsqrt(jnp.mean(flattened * flattened, axis=0, keepdims=True) + 1e-06)
    unit_rows = (flattened * norm_factor).astype(jnp.bfloat16).T
    following = passed_along(unit_rows, "feat", -1)
    partner = from_partner(unit_rows, "rows", 0)
    following_partner = from_partner(following, "rows", 0)
    candidates = jnp.stack([unit_rows, following, partner, following_partner])
    tile_total = tile_blocks.shape[2]
    own_list = lax.dynamic_index_in_dim(tile_blocks[:, 0, :], row_place, 0, keepdims=False)
    own_count = lax.dynamic_index_in_dim(tile_counts[:, 0], row_place, 0, keepdims=False)

    def add_tile(slot_index, buffer):
        block_id = own_list[slot_index]
        other_half = (block_id // groups != row_place).astype(jnp.int32)
        other_bucket = (block_id % groups != feat_place).astype(jnp.int32)
        keyed_block = lax.dynamic_index_in_dim(
            candidates, other_bucket + 2 * other_half, 0, keepdims=False
        )
        tile_value = (
            lax.dot_general(
                unit_rows, keyed_block, (((1,), (1,)), ((), ())), preferred_element_type=jnp.float32
            )
            * score_scale
        )
        return lax.dynamic_update_index_in_dim(buffer, tile_value, slot_index, 0)

    empty_tiles = jnp.zeros((tile_total, block_rows, block_rows), jnp.float32)
    result = lax.fori_loop(0, own_count, add_tile, empty_tiles)
    return (result[None, None], unit_rows[None])


ACROSS = 2
ALONG = 4


def signs_kernel(signs_ref, wide_ref):
    step = signs_ref.shape[1]
    for i in range(signs_ref.shape[0]):
        tile = jnp.broadcast_to(signs_ref[i : i + 1, :].astype(jnp.float32), (step, step))
        tile = tile.T.astype(jnp.bfloat16)
        for low in range(0, wide_ref.shape[1], step):
            wide_ref[i * step : (i + 1) * step, low : low + step] = tile


def wanted(hop):
    place = lax.axis_index("feat")
    side = lax.rem(place, ACROSS)
    first = ACROSS * lax.bitwise_xor(lax.div(place, ACROSS), hop)
    last = lax.rem(first + ACROSS, ACROSS * ALONG)
    return jnp.where(side == 0, first, last), first + 1, jnp.where(side == 0, last, first)


KEPT, MIDDLE, OTHER = range(3)
ROUTED_FIRST = (((0, MIDDLE), (0, OTHER)), ((1, MIDDLE), (1, OTHER)), ((2, MIDDLE), (2, OTHER)), ((3, OTHER),))
ROUTED_LATER = (((0, KEPT),), ((1, KEPT),), ((2, KEPT),), ((3, KEPT),), ((3, MIDDLE),))


def route_kernel(groups, emb_ref, *refs):
    first_call = groups is ROUTED_FIRST
    signs_ref, refs = refs[0], list(refs[1:])
    if first_call:
        sign_sem, sign_rows = refs.pop(), refs.pop()
        sign_copy = pltpu.make_async_copy(signs_ref, sign_rows, sign_sem)
        sign_copy.start()
    sems = refs.pop()
    wide_ref = refs.pop() if first_call else signs_ref
    targets = []
    for ref, blocks in zip(refs, groups):
        for i, (hop, kind) in enumerate(blocks):
            targets.append((ref.at[i] if len(blocks) > 1 else ref, wanted(hop)[kind]))
    copies = []
    for i, (ref, block) in enumerate(targets):
        rows = ref.shape[1]
        start = pl.multiple_of(block * rows, rows)
        copies.append(pltpu.make_async_copy(emb_ref.at[:, pl.ds(start, rows)], ref, sems.at[i]))
    for copy in copies:
        copy.start()
    if first_call:
        sign_copy.wait()
        signs_kernel(sign_rows, wide_ref)
    for copy, (ref, block) in zip(copies, targets):
        copy.wait()
        ref[...] = ref[...] * wide_ref[...]


def route(embeddings, signs, rows, groups):
    width = embeddings.shape[0]
    first_call = groups is ROUTED_FIRST
    shapes = [(width, rows) if len(blocks) == 1 else (len(blocks), width, rows) for blocks in groups]
    count = sum(len(blocks) for blocks in groups)
    scratch = [pltpu.SemaphoreType.DMA((count,))]
    if first_call:
        shapes.append((width, rows))
        signs = signs.reshape(width // 128, 128)
        scratch += [pltpu.VMEM(signs.shape, signs.dtype), pltpu.SemaphoreType.DMA]
        signs = pltpu.with_memory_space_constraint(signs, pltpu.HBM)
    return pl.pallas_call(
        functools.partial(route_kernel, groups),
        in_specs=[HBM, HBM if first_call else VMEM],
        out_specs=[VMEM] * len(shapes),
        out_shape=[jax.ShapeDtypeStruct(shape, jnp.bfloat16) for shape in shapes],
        scratch_shapes=scratch,
        compiler_params=pltpu.CompilerParams(vmem_limit_bytes=VMEM_LIMIT),
        cost_estimate=pl.CostEstimate(
            flops=count * width * rows, bytes_accessed=count * width * rows * 4, transcendentals=0
        ),
        name="route",
    )(pltpu.with_memory_space_constraint(embeddings, pltpu.HBM), signs)


def butterfly(parts):
    parts = list(parts)
    half = 1
    while half < len(parts):
        for low in range(0, len(parts), 2 * half):
            for i in range(low, low + half):
                a, b = parts[i], parts[i + half]
                parts[i], parts[i + half] = a + b, a - b
        half *= 2
    return parts


def turned_parts(pieces, table_ref, low, chunk):
    return butterfly(
        lax.dot_general(
            piece,
            table_ref[:, low : low + chunk],
            (((0,), (0,)), ((), ())),
            preferred_element_type=jnp.float32,
        )
        for piece in pieces
    )


def begin_kernel(picks, *refs):
    table_ref, out_ref = refs[-2:]
    place = lax.axis_index("feat")
    pieces = [pick(refs, place) for pick in picks]
    width = pieces[0].shape[0]
    chunk = 256
    for low in range(0, width, chunk):
        for i, part in enumerate(turned_parts(pieces, table_ref, low, chunk)):
            out_ref[:, i * width + low : i * width + low + chunk] = part


def begin(inputs, picks, table):
    count = len(picks)
    width, rows = inputs[0].shape[-2:]
    return pl.pallas_call(
        functools.partial(begin_kernel, picks),
        in_specs=[VMEM] * (len(inputs) + 1),
        out_specs=VMEM,
        out_shape=jax.ShapeDtypeStruct((rows, count * width), jnp.float32),
        compiler_params=pltpu.CompilerParams(vmem_limit_bytes=VMEM_LIMIT),
        cost_estimate=pl.CostEstimate(
            flops=2 * rows * count * width * width, bytes_accessed=3 << 20, transcendentals=0
        ),
        name="begin",
    )(*inputs, table)


def finish_kernel(picks, *refs):
    begun_ref, table_ref, out_ref, turned = refs[-4:]
    place = lax.axis_index("feat")
    pieces = [pick(refs, place) for pick in picks]
    width, rows = pieces[0].shape
    half = len(pieces)
    count = 2 * half
    features = count * width
    chunk = 256
    total = jnp.zeros((rows, 128), jnp.float32)
    for low in range(0, width, chunk):
        for i, late in enumerate(turned_parts(pieces, table_ref, low, chunk)):
            early = begun_ref[:, i * width + low : i * width + low + chunk]
            for place_out, part in ((i, early + late), (i + half, early - late)):
                turned[:, place_out * width + low : place_out * width + low + chunk] = part
                square = part * part
                for lane in range(0, chunk, 128):
                    total = total + square[:, lane : lane + 128]
    mean = jnp.sum(total, axis=1, keepdims=True) * (1.0 / (features * features))
    factor = lax.rsqrt(mean + 1e-06) * (1.0 / math.sqrt(features))
    for i in range(count):
        odd = jnp.int32(0)
        for bit in range(count.bit_length() - 1):
            if i >> bit & 1:
                odd = odd + (lax.shift_right_logical(place, bit) & 1)
        sign = (1 - 2 * (odd & 1)).astype(jnp.float32)
        columns = slice(i * width, (i + 1) * width)
        out_ref[:, columns] = (turned[:, columns] * (factor * sign)).astype(jnp.bfloat16)


def finish(inputs, picks, begun, table):
    count = 2 * len(picks)
    width, rows = inputs[0].shape[-2:]
    return pl.pallas_call(
        functools.partial(finish_kernel, picks),
        in_specs=[VMEM] * (len(inputs) + 2),
        out_specs=VMEM,
        out_shape=jax.ShapeDtypeStruct((rows, count * width), jnp.bfloat16),
        scratch_shapes=[pltpu.VMEM((rows, count * width), jnp.float32)],
        compiler_params=pltpu.CompilerParams(vmem_limit_bytes=VMEM_LIMIT),
        cost_estimate=pl.CostEstimate(
            flops=rows * count * width * width, bytes_accessed=5 << 20, transcendentals=0
        ),
        name="finish",
    )(*inputs, begun, table)


def listed(lists_ref, counts_ref, slot, groups):
    place = lax.axis_index("feat")
    half = lax.axis_index("rows")
    block_id = lists_ref[half, slot]
    other_half = (lax.div(block_id, groups) != half).astype(jnp.int32)
    own_bucket = (lax.rem(block_id, groups) == place).astype(jnp.int32)
    side = lax.rem(place, ACROSS)
    is_outer = (own_bucket != side).astype(jnp.int32)
    choice = is_outer + 2 * other_half
    return jnp.where(slot < counts_ref[half], choice, -1)


def product(query, key, features):
    return lax.dot_general(
        query, key, (((1,), (1,)), ((), ())), preferred_element_type=jnp.float32
    ) * (1.0 / math.sqrt(features))


def early_kernel(groups, lists_ref, counts_ref, mid_ref, outer_ref, mid2_ref, tiles_ref, unit_ref, out_sem):
    own_middle = lax.rem(lax.axis_index("feat"), ACROSS) == 1
    features = mid_ref.shape[1]
    keys = (mid_ref, outer_ref, mid2_ref)
    for value, query_ref in ((True, mid_ref), (False, outer_ref)):

        @pl.when(own_middle == value)
        def _(query_ref=query_ref):
            pltpu.make_async_copy(query_ref, unit_ref, out_sem).start()

    def fill(slot, carry):
        choice = listed(lists_ref, counts_ref, slot, groups)

        @pl.when((choice < 0) | (choice > 2))
        def _():
            tiles_ref[slot] = jnp.zeros(tiles_ref.shape[1:], jnp.float32)

        for value, query_ref in ((True, mid_ref), (False, outer_ref)):
            for index, key_ref in enumerate(keys):

                @pl.when((own_middle == value) & (choice == index))
                def _(query_ref=query_ref, key_ref=key_ref):
                    tiles_ref[slot] = product(query_ref[...], key_ref[...], features)

        return carry

    lax.fori_loop(0, tiles_ref.shape[0], fill, 0)
    pltpu.make_async_copy(mid_ref, unit_ref, out_sem).wait()


def late_kernel(groups, lists_ref, counts_ref, mid_ref, outer_ref, outer2_ref, early_ref, tiles_ref, tile, out_sem):
    own_middle = lax.rem(lax.axis_index("feat"), ACROSS) == 1
    features = mid_ref.shape[1]
    choices = [listed(lists_ref, counts_ref, slot, groups) for slot in range(early_ref.shape[0])]
    needed = functools.reduce(jnp.logical_or, [choice == 3 for choice in choices])
    slot = jnp.int32(0)
    for i, choice in enumerate(choices):
        slot = jnp.where(choice == 3, i, slot)
    for value, query_ref in ((True, mid_ref), (False, outer_ref)):

        @pl.when((own_middle == value) & needed)
        def _(query_ref=query_ref):
            tile[...] = product(query_ref[...], outer2_ref[...], features)

    @pl.when(needed)
    def _():
        out = pltpu.make_async_copy(tile, tiles_ref.at[slot], out_sem)
        out.start()
        out.wait()


def scores_early(lists, counts, mid, outer, mid2, groups):
    rows, features = mid.shape
    tiles = lists.shape[1]
    return pl.pallas_call(
        functools.partial(early_kernel, groups),
        in_specs=[SMEM, SMEM, VMEM, VMEM, VMEM],
        out_specs=[VMEM, HBM],
        out_shape=[
            jax.ShapeDtypeStruct((tiles, rows, rows), jnp.float32),
            jax.ShapeDtypeStruct((rows, features), jnp.bfloat16),
        ],
        scratch_shapes=[pltpu.SemaphoreType.DMA],
        compiler_params=pltpu.CompilerParams(vmem_limit_bytes=VMEM_LIMIT),
        cost_estimate=pl.CostEstimate(
            flops=4 * rows * rows * features, bytes_accessed=9 << 20, transcendentals=0
        ),
        name="early",
    )(lists, counts, mid, outer, mid2)


def scores_late(lists, counts, mid, outer, outer2, early, groups):
    rows, features = mid.shape
    return pl.pallas_call(
        functools.partial(late_kernel, groups),
        in_specs=[SMEM, SMEM, VMEM, VMEM, VMEM, HBM],
        out_specs=HBM,
        out_shape=jax.ShapeDtypeStruct(early.shape, early.dtype),
        scratch_shapes=[pltpu.VMEM((rows, rows), jnp.float32), pltpu.SemaphoreType.DMA],
        input_output_aliases={5: 0},
        compiler_params=pltpu.CompilerParams(vmem_limit_bytes=VMEM_LIMIT),
        cost_estimate=pl.CostEstimate(
            flops=2 * rows * rows * features, bytes_accessed=4 << 20, transcendentals=0
        ),
        name="late",
    )(lists, counts, mid, outer, outer2, early)


ORDER = (
    ("S2",),
    ("O3",),
    ("X0",),
    ("S1",),
    ("X1",),
    ("X2",),
    ("K1", "X0"),
    ("R2", "K0"),
    ("B3", "S2"),
    ("K3", "X1"),
    ("R3", "R2"),
    ("XO", "R2"),
    ("XB", "K1"),
    ("K2", "R3"),
)


ROUTE_AFTER = "S1"
MIDDLE_AFTER = ("K3", "R3")


def after(value, *events):
    return lax.optimization_barrier((value, *events))[0]


def chip(at, side):
    return ACROSS * at + side


EVERY = tuple(range(ACROSS * ALONG))
DIRECT = (chip(0, 0), chip(1, 1), chip(2, 0), chip(3, 1))
RELAYED = (chip(1, 0), chip(0, 1), chip(3, 0), chip(2, 1))
NEAR = 1
FAR = (2, 3)


def hop_over(value, axis, mask, receivers=None):
    if receivers is None:
        receivers = range(lax.axis_size(axis))
    return lax.ppermute(value, axis, [(to ^ mask, to) for to in receivers])


def along(value, hop, receivers=EVERY):
    return hop_over(value, "feat", ACROSS * hop, receivers)


def across(value):
    return hop_over(value, "feat", 1)


def plain(index, pick=None):
    if pick is None:
        return lambda refs, place: refs[index][...]
    return lambda refs, place: refs[index][pick]


def kept_far(direct, relayed):
    def read(refs, place):
        straight = lax.rem(lax.div(place, ACROSS) + lax.rem(place, ACROSS), 2) == 0
        return jnp.where(straight, refs[direct][...], refs[relayed][...])

    return read


def paired(embeddings, signs, tile_blocks, tile_counts):
    groups = lax.axis_size("feat")
    width, columns = embeddings.shape
    rows = columns // groups
    table = jnp.asarray(parity_table(width), jnp.bfloat16)
    S0, S1, S2, O3, wide = route(embeddings, signs, rows, ROUTED_FIRST)
    late = {}
    plan = {
        "S1": lambda got: (S1, along, 1),
        "S2": lambda got: (S2, along, 2),
        "B3": lambda got: (late["B3"], along, 3),
        "O3": lambda got: (O3, along, 3),
        "K1": lambda got: (late["K1"], along, 1),
        "K2": lambda got: (late["K2"], along, 2, DIRECT),
        "K3": lambda got: (late["K3"], along, 3, DIRECT),
        "X0": lambda got: (S0, across),
        "X1": lambda got: (got["S1"], across),
        "X2": lambda got: (got["S2"], across),
        "XB": lambda got: (got["B3"], across),
        "XO": lambda got: (got["O3"], across),
        "R2": lambda got: (got["S2"][1], along, NEAR, RELAYED),
        "R3": lambda got: (got["O3"], along, NEAR, RELAYED),
    }
    got = {}
    for name, *events in ORDER:
        if not late and ROUTE_AFTER in got:
            rest = route(embeddings, after(wide, got[ROUTE_AFTER]), rows, ROUTED_LATER)
            late = dict(zip(("K0", "K1", "K2", "K3", "B3"), rest))
        value, move, *rest = plan[name](got)
        if events:
            value = after(value, *(got.get(event, late.get(event)) for event in events))
        with jax.named_scope(name):
            got[name] = move(value, *rest)
    mid_begun = begin(
        [S0, got["X0"], got["S1"], got["X1"]], [plain(i, 0) for i in range(4)], table
    )
    outer_begun = begin(
        [late["K0"], got["X0"], got["K1"], got["X1"]],
        [plain(0), plain(1, 1), plain(2), plain(3, 1)],
        table,
    )
    first = after(got["S2"], *(got[name] for name in MIDDLE_AFTER))
    mid = finish(
        [first, got["X2"], got["B3"], got["XB"]],
        [plain(0, 0), plain(1, 0), plain(2), plain(3)],
        mid_begun,
        table,
    )
    mid2 = hop_over(mid, "rows", 1)
    outer = finish(
        [got["K2"], got["R3"], got["X2"], got["K3"], got["R2"], got["XO"]],
        [kept_far(0, 1), plain(2, 1), kept_far(3, 4), plain(5)],
        outer_begun,
        table,
    )
    outer2 = hop_over(outer, "rows", 1)
    lists = tile_blocks[:, 0, :]
    counts = tile_counts[:, 0]
    early, unit = scores_early(lists, counts, mid, outer, mid2, groups)
    tiles = scores_late(lists, counts, mid, outer, outer2, early, groups)
    return (tiles[None, None], unit[None])


def solution(mesh):
    body = paired if mesh.shape["feat"] == ALONG * ACROSS and mesh.shape["rows"] == 2 else general
    return jax.shard_map(
        body,
        mesh=mesh,
        in_specs=(
            P("feat", ("groups", "rows")),
            P("feat"),
            P("groups", "feat", None),
            P("groups", "feat"),
        ),
        out_specs=(
            P(("groups", "rows"), "feat", None, None, None),
            P(("groups", "rows"), "feat", None),
        ),
        check_vma=False,
    )
```

```python
import functools
import math

import jax
import jax.numpy as jnp
import numpy as np
from jax import lax
from jax.experimental import pallas as pl
from jax.experimental.pallas import tpu as pltpu
from jax.sharding import PartitionSpec as P

SMEM = pl.BlockSpec(memory_space=pltpu.SMEM)
VMEM = pl.BlockSpec(memory_space=pltpu.VMEM)
HBM = pl.BlockSpec(memory_space=pltpu.HBM)
VMEM_LIMIT = 24 << 20


def parity_table(length):
    positions = np.arange(length)
    shared = positions[:, None] & positions[None, :]
    parity = np.zeros_like(shared)
    while shared.any():
        parity ^= shared & 1
        shared = shared >> 1
    return 1 - 2 * parity


def from_partner(block, axis, distance):
    count = lax.axis_size(axis)
    route = []
    for low in range(count):
        high = low | 1 << distance
        if high != low and high < count:
            route += [(low, high), (high, low)]
    return lax.ppermute(block, axis, route)


def passed_along(value, axis, steps):
    count = lax.axis_size(axis)
    pairs = [(source, (source + steps) % count) for source in range(count)]
    return lax.ppermute(value, axis, pairs)


def general(embeddings, signs, tile_blocks, tile_counts):
    groups = lax.axis_size("feat")
    feat_place = lax.axis_index("feat")
    row_place = lax.axis_index("rows")
    signed = embeddings * signs.astype(jnp.bfloat16)[:, None]
    regrouped = lax.all_to_all(signed, "feat", split_axis=1, concat_axis=0, tiled=True)
    features = regrouped.shape[0]
    block_rows = regrouped.shape[1]
    local_width = features // groups
    score_scale = 1.0 / math.sqrt(features)
    inner_table = jnp.asarray(parity_table(local_width), jnp.bfloat16)
    outer_table = jnp.asarray(parity_table(groups), jnp.float32)
    blocked = regrouped.reshape(groups, local_width, block_rows)
    first_section = jnp.einsum(
        "abr,bc->acr", blocked, inner_table, preferred_element_type=jnp.float32
    )
    turned = (
        jnp.einsum("acr,ad->dcr", first_section, outer_table, precision=lax.Precision.HIGHEST)
        * score_scale
    )
    flattened = turned.reshape(features, block_rows)
    norm_factor = lax.rsqrt(jnp.mean(flattened * flattened, axis=0, keepdims=True) + 1e-06)
    unit_rows = (flattened * norm_factor).astype(jnp.bfloat16).T
    following = passed_along(unit_rows, "feat", -1)
    partner = from_partner(unit_rows, "rows", 0)
    following_partner = from_partner(following, "rows", 0)
    candidates = jnp.stack([unit_rows, following, partner, following_partner])
    tile_total = tile_blocks.shape[2]
    own_list = lax.dynamic_index_in_dim(tile_blocks[:, 0, :], row_place, 0, keepdims=False)
    own_count = lax.dynamic_index_in_dim(tile_counts[:, 0], row_place, 0, keepdims=False)

    def add_tile(slot_index, buffer):
        block_id = own_list[slot_index]
        other_half = (block_id // groups != row_place).astype(jnp.int32)
        other_bucket = (block_id % groups != feat_place).astype(jnp.int32)
        keyed_block = lax.dynamic_index_in_dim(
            candidates, other_bucket + 2 * other_half, 0, keepdims=False
        )
        tile_value = (
            lax.dot_general(
                unit_rows, keyed_block, (((1,), (1,)), ((), ())), preferred_element_type=jnp.float32
            )
            * score_scale
        )
        return lax.dynamic_update_index_in_dim(buffer, tile_value, slot_index, 0)

    empty_tiles = jnp.zeros((tile_total, block_rows, block_rows), jnp.float32)
    result = lax.fori_loop(0, own_count, add_tile, empty_tiles)
    return (result[None, None], unit_rows[None])


ACROSS = 2
ALONG = 4


def signs_kernel(signs_ref, wide_ref):
    step = signs_ref.shape[1]
    for i in range(signs_ref.shape[0]):
        tile = jnp.broadcast_to(signs_ref[i : i + 1, :].astype(jnp.float32), (step, step))
        tile = tile.T.astype(jnp.bfloat16)
        for low in range(0, wide_ref.shape[1], step):
            wide_ref[i * step : (i + 1) * step, low : low + step] = tile


def wanted(hop):
    place = lax.axis_index("feat")
    side = lax.rem(place, ACROSS)
    first = ACROSS * lax.bitwise_xor(lax.div(place, ACROSS), hop)
    last = lax.rem(first + ACROSS, ACROSS * ALONG)
    return jnp.where(side == 0, first, last), first + 1, jnp.where(side == 0, last, first)


KEPT, MIDDLE, OTHER = range(3)
ROUTED_FIRST = (((0, MIDDLE), (0, OTHER)), ((1, MIDDLE), (1, OTHER)), ((2, MIDDLE), (2, OTHER)), ((3, OTHER),))
ROUTED_LATER = (((0, KEPT),), ((1, KEPT),), ((2, KEPT),), ((3, KEPT),), ((3, MIDDLE),))


def route_kernel(groups, emb_ref, *refs):
    first_call = groups is ROUTED_FIRST
    signs_ref, refs = refs[0], list(refs[1:])
    if first_call:
        sign_sem, sign_rows = refs.pop(), refs.pop()
        sign_copy = pltpu.make_async_copy(signs_ref, sign_rows, sign_sem)
        sign_copy.start()
    sems = refs.pop()
    wide_ref = refs.pop() if first_call else signs_ref
    targets = []
    for ref, blocks in zip(refs, groups):
        for i, (hop, kind) in enumerate(blocks):
            targets.append((ref.at[i] if len(blocks) > 1 else ref, wanted(hop)[kind]))
    copies = []
    for i, (ref, block) in enumerate(targets):
        rows = ref.shape[1]
        start = pl.multiple_of(block * rows, rows)
        copies.append(pltpu.make_async_copy(emb_ref.at[:, pl.ds(start, rows)], ref, sems.at[i]))
    for copy in copies:
        copy.start()
    if first_call:
        sign_copy.wait()
        signs_kernel(sign_rows, wide_ref)
    for copy, (ref, block) in zip(copies, targets):
        copy.wait()
        ref[...] = ref[...] * wide_ref[...]


def route(embeddings, signs, rows, groups):
    width = embeddings.shape[0]
    first_call = groups is ROUTED_FIRST
    shapes = [(width, rows) if len(blocks) == 1 else (len(blocks), width, rows) for blocks in groups]
    count = sum(len(blocks) for blocks in groups)
    scratch = [pltpu.SemaphoreType.DMA((count,))]
    if first_call:
        shapes.append((width, rows))
        signs = signs.reshape(width // 128, 128)
        scratch += [pltpu.VMEM(signs.shape, signs.dtype), pltpu.SemaphoreType.DMA]
        signs = pltpu.with_memory_space_constraint(signs, pltpu.HBM)
    return pl.pallas_call(
        functools.partial(route_kernel, groups),
        in_specs=[HBM, HBM if first_call else VMEM],
        out_specs=[VMEM] * len(shapes),
        out_shape=[jax.ShapeDtypeStruct(shape, jnp.bfloat16) for shape in shapes],
        scratch_shapes=scratch,
        compiler_params=pltpu.CompilerParams(vmem_limit_bytes=VMEM_LIMIT),
        cost_estimate=pl.CostEstimate(
            flops=count * width * rows, bytes_accessed=count * width * rows * 4, transcendentals=0
        ),
        name="route",
    )(pltpu.with_memory_space_constraint(embeddings, pltpu.HBM), signs)


def butterfly(parts):
    parts = list(parts)
    half = 1
    while half < len(parts):
        for low in range(0, len(parts), 2 * half):
            for i in range(low, low + half):
                a, b = parts[i], parts[i + half]
                parts[i], parts[i + half] = a + b, a - b
        half *= 2
    return parts


def turned_parts(pieces, table_ref):
    half = table_ref.shape[0]
    pairs = []
    for piece in pieces:
        low, high = (
            lax.dot_general(
                piece[at : at + half],
                table_ref[...],
                (((0,), (0,)), ((), ())),
                preferred_element_type=jnp.float32,
            )
            for at in (0, half)
        )
        pairs.append((low + high, low - high))
    return [(side * half, butterfly(pair[side] for pair in pairs)) for side in range(2)]


def begin_kernel(picks, *refs):
    table_ref, out_ref = refs[-2:]
    place = lax.axis_index("feat")
    pieces = [pick(refs, place) for pick in picks]
    width = pieces[0].shape[0]
    chunk = width // 2
    for low, parts in turned_parts(pieces, table_ref):
        for i, part in enumerate(parts):
            out_ref[:, i * width + low : i * width + low + chunk] = part


def begin(inputs, picks, table):
    count = len(picks)
    width, rows = inputs[0].shape[-2:]
    return pl.pallas_call(
        functools.partial(begin_kernel, picks),
        in_specs=[VMEM] * (len(inputs) + 1),
        out_specs=VMEM,
        out_shape=jax.ShapeDtypeStruct((rows, count * width), jnp.float32),
        compiler_params=pltpu.CompilerParams(vmem_limit_bytes=VMEM_LIMIT),
        cost_estimate=pl.CostEstimate(
            flops=2 * rows * count * width * width, bytes_accessed=3 << 20, transcendentals=0
        ),
        name="begin",
    )(*inputs, table)


def finish_kernel(picks, *refs):
    begun_ref, table_ref, out_ref, turned = refs[-4:]
    place = lax.axis_index("feat")
    pieces = [pick(refs, place) for pick in picks]
    width, rows = pieces[0].shape
    half = len(pieces)
    count = 2 * half
    features = count * width
    chunk = width // 2
    total = jnp.zeros((rows, 128), jnp.float32)
    for low, parts in turned_parts(pieces, table_ref):
        for i, late in enumerate(parts):
            early = begun_ref[:, i * width + low : i * width + low + chunk]
            for place_out, part in ((i, early + late), (i + half, early - late)):
                turned[:, place_out * width + low : place_out * width + low + chunk] = part
                square = part * part
                for lane in range(0, chunk, 128):
                    total = total + square[:, lane : lane + 128]
    mean = jnp.sum(total, axis=1, keepdims=True) * (1.0 / (features * features))
    factor = lax.rsqrt(mean + 1e-06) * (1.0 / math.sqrt(features))
    for i in range(count):
        odd = jnp.int32(0)
        for bit in range(count.bit_length() - 1):
            if i >> bit & 1:
                odd = odd + (lax.shift_right_logical(place, bit) & 1)
        sign = (1 - 2 * (odd & 1)).astype(jnp.float32)
        columns = slice(i * width, (i + 1) * width)
        out_ref[:, columns] = (turned[:, columns] * (factor * sign)).astype(jnp.bfloat16)


def finish(inputs, picks, begun, table):
    count = 2 * len(picks)
    width, rows = inputs[0].shape[-2:]
    return pl.pallas_call(
        functools.partial(finish_kernel, picks),
        in_specs=[VMEM] * (len(inputs) + 2),
        out_specs=VMEM,
        out_shape=jax.ShapeDtypeStruct((rows, count * width), jnp.bfloat16),
        scratch_shapes=[pltpu.VMEM((rows, count * width), jnp.float32)],
        compiler_params=pltpu.CompilerParams(vmem_limit_bytes=VMEM_LIMIT),
        cost_estimate=pl.CostEstimate(
            flops=rows * count * width * width, bytes_accessed=5 << 20, transcendentals=0
        ),
        name="finish",
    )(*inputs, begun, table)


def listed(lists_ref, counts_ref, slot, groups):
    place = lax.axis_index("feat")
    half = lax.axis_index("rows")
    block_id = lists_ref[half, slot]
    other_half = (lax.div(block_id, groups) != half).astype(jnp.int32)
    own_bucket = (lax.rem(block_id, groups) == place).astype(jnp.int32)
    side = lax.rem(place, ACROSS)
    is_outer = (own_bucket != side).astype(jnp.int32)
    choice = is_outer + 2 * other_half
    return jnp.where(slot < counts_ref[half], choice, -1)


def product(query, key, features):
    return lax.dot_general(
        query, key, (((1,), (1,)), ((), ())), preferred_element_type=jnp.float32
    ) * (1.0 / math.sqrt(features))


def early_kernel(groups, lists_ref, counts_ref, mid_ref, outer_ref, mid2_ref, tiles_ref, unit_ref, out_sem):
    own_middle = lax.rem(lax.axis_index("feat"), ACROSS) == 1
    features = mid_ref.shape[1]
    keys = (mid_ref, outer_ref, mid2_ref)
    for value, query_ref in ((True, mid_ref), (False, outer_ref)):

        @pl.when(own_middle == value)
        def _(query_ref=query_ref):
            pltpu.make_async_copy(query_ref, unit_ref, out_sem).start()

    def fill(slot, carry):
        choice = listed(lists_ref, counts_ref, slot, groups)

        @pl.when((choice < 0) | (choice > 2))
        def _():
            tiles_ref[slot] = jnp.zeros(tiles_ref.shape[1:], jnp.float32)

        for value, query_ref in ((True, mid_ref), (False, outer_ref)):
            for index, key_ref in enumerate(keys):

                @pl.when((own_middle == value) & (choice == index))
                def _(query_ref=query_ref, key_ref=key_ref):
                    tiles_ref[slot] = product(query_ref[...], key_ref[...], features)

        return carry

    lax.fori_loop(0, tiles_ref.shape[0], fill, 0)
    pltpu.make_async_copy(mid_ref, unit_ref, out_sem).wait()


def late_kernel(groups, lists_ref, counts_ref, mid_ref, outer_ref, outer2_ref, early_ref, tiles_ref, tile, out_sem):
    own_middle = lax.rem(lax.axis_index("feat"), ACROSS) == 1
    features = mid_ref.shape[1]
    choices = [listed(lists_ref, counts_ref, slot, groups) for slot in range(early_ref.shape[0])]
    needed = functools.reduce(jnp.logical_or, [choice == 3 for choice in choices])
    slot = jnp.int32(0)
    for i, choice in enumerate(choices):
        slot = jnp.where(choice == 3, i, slot)
    for value, query_ref in ((True, mid_ref), (False, outer_ref)):

        @pl.when((own_middle == value) & needed)
        def _(query_ref=query_ref):
            tile[...] = product(query_ref[...], outer2_ref[...], features)

    @pl.when(needed)
    def _():
        out = pltpu.make_async_copy(tile, tiles_ref.at[slot], out_sem)
        out.start()
        out.wait()


def scores_early(lists, counts, mid, outer, mid2, groups):
    rows, features = mid.shape
    tiles = lists.shape[1]
    return pl.pallas_call(
        functools.partial(early_kernel, groups),
        in_specs=[SMEM, SMEM, VMEM, VMEM, VMEM],
        out_specs=[VMEM, HBM],
        out_shape=[
            jax.ShapeDtypeStruct((tiles, rows, rows), jnp.float32),
            jax.ShapeDtypeStruct((rows, features), jnp.bfloat16),
        ],
        scratch_shapes=[pltpu.SemaphoreType.DMA],
        compiler_params=pltpu.CompilerParams(vmem_limit_bytes=VMEM_LIMIT),
        cost_estimate=pl.CostEstimate(
            flops=4 * rows * rows * features, bytes_accessed=9 << 20, transcendentals=0
        ),
        name="early",
    )(lists, counts, mid, outer, mid2)


def scores_late(lists, counts, mid, outer, outer2, early, groups):
    rows, features = mid.shape
    return pl.pallas_call(
        functools.partial(late_kernel, groups),
        in_specs=[SMEM, SMEM, VMEM, VMEM, VMEM, HBM],
        out_specs=HBM,
        out_shape=jax.ShapeDtypeStruct(early.shape, early.dtype),
        scratch_shapes=[pltpu.VMEM((rows, rows), jnp.float32), pltpu.SemaphoreType.DMA],
        input_output_aliases={5: 0},
        compiler_params=pltpu.CompilerParams(vmem_limit_bytes=VMEM_LIMIT),
        cost_estimate=pl.CostEstimate(
            flops=2 * rows * rows * features, bytes_accessed=4 << 20, transcendentals=0
        ),
        name="late",
    )(lists, counts, mid, outer, outer2, early)


ORDER = (
    ("S2",),
    ("O3",),
    ("X0",),
    ("S1",),
    ("X1",),
    ("X2",),
    ("K1", "X0"),
    ("R2", "K0"),
    ("B3", "S2"),
    ("K3", "X1"),
    ("R3", "R2"),
    ("XO", "R2"),
    ("XB", "K1"),
    ("K2", "R3"),
)


ROUTE_AFTER = "S1"
MIDDLE_AFTER = ("K3", "R3")


def after(value, *events):
    return lax.optimization_barrier((value, *events))[0]


def chip(at, side):
    return ACROSS * at + side


EVERY = tuple(range(ACROSS * ALONG))
DIRECT = (chip(0, 0), chip(1, 1), chip(2, 0), chip(3, 1))
RELAYED = (chip(1, 0), chip(0, 1), chip(3, 0), chip(2, 1))
NEAR = 1
FAR = (2, 3)


def hop_over(value, axis, mask, receivers=None):
    if receivers is None:
        receivers = range(lax.axis_size(axis))
    return lax.ppermute(value, axis, [(to ^ mask, to) for to in receivers])


def along(value, hop, receivers=EVERY):
    return hop_over(value, "feat", ACROSS * hop, receivers)


def across(value):
    return hop_over(value, "feat", 1)


def plain(index, pick=None):
    if pick is None:
        return lambda refs, place: refs[index][...]
    return lambda refs, place: refs[index][pick]


def kept_far(direct, relayed):
    def read(refs, place):
        straight = lax.rem(lax.div(place, ACROSS) + lax.rem(place, ACROSS), 2) == 0
        return jnp.where(straight, refs[direct][...], refs[relayed][...])

    return read


def paired(embeddings, signs, tile_blocks, tile_counts):
    groups = lax.axis_size("feat")
    width, columns = embeddings.shape
    rows = columns // groups
    table = jnp.asarray(parity_table(width // 2), jnp.bfloat16)
    S0, S1, S2, O3, wide = route(embeddings, signs, rows, ROUTED_FIRST)
    late = {}
    plan = {
        "S1": lambda got: (S1, along, 1),
        "S2": lambda got: (S2, along, 2),
        "B3": lambda got: (late["B3"], along, 3),
        "O3": lambda got: (O3, along, 3),
        "K1": lambda got: (late["K1"], along, 1),
        "K2": lambda got: (late["K2"], along, 2, DIRECT),
        "K3": lambda got: (late["K3"], along, 3, DIRECT),
        "X0": lambda got: (S0, across),
        "X1": lambda got: (got["S1"], across),
        "X2": lambda got: (got["S2"], across),
        "XB": lambda got: (got["B3"], across),
        "XO": lambda got: (got["O3"], across),
        "R2": lambda got: (got["S2"][1], along, NEAR, RELAYED),
        "R3": lambda got: (got["O3"], along, NEAR, RELAYED),
    }
    got = {}
    for name, *events in ORDER:
        if not late and ROUTE_AFTER in got:
            rest = route(embeddings, after(wide, got[ROUTE_AFTER]), rows, ROUTED_LATER)
            late = dict(zip(("K0", "K1", "K2", "K3", "B3"), rest))
        value, move, *rest = plan[name](got)
        if events:
            value = after(value, *(got.get(event, late.get(event)) for event in events))
        with jax.named_scope(name):
            got[name] = move(value, *rest)
    mid_begun = begin(
        [S0, got["X0"], got["S1"], got["X1"]], [plain(i, 0) for i in range(4)], table
    )
    outer_begun = begin(
        [late["K0"], got["X0"], got["K1"], got["X1"]],
        [plain(0), plain(1, 1), plain(2), plain(3, 1)],
        table,
    )
    first = after(got["S2"], *(got[name] for name in MIDDLE_AFTER))
    mid = finish(
        [first, got["X2"], got["B3"], got["XB"]],
        [plain(0, 0), plain(1, 0), plain(2), plain(3)],
        mid_begun,
        table,
    )
    mid2 = hop_over(mid, "rows", 1)
    outer = finish(
        [got["K2"], got["R3"], got["X2"], got["K3"], got["R2"], got["XO"]],
        [kept_far(0, 1), plain(2, 1), kept_far(3, 4), plain(5)],
        outer_begun,
        table,
    )
    outer2 = hop_over(outer, "rows", 1)
    lists = tile_blocks[:, 0, :]
    counts = tile_counts[:, 0]
    early, unit = scores_early(lists, counts, mid, outer, mid2, groups)
    tiles = scores_late(lists, counts, mid, outer, outer2, early, groups)
    return (tiles[None, None], unit[None])


def solution(mesh):
    body = paired if mesh.shape["feat"] == ALONG * ACROSS and mesh.shape["rows"] == 2 else general
    return jax.shard_map(
        body,
        mesh=mesh,
        in_specs=(
            P("feat", ("groups", "rows")),
            P("feat"),
            P("groups", "feat", None),
            P("groups", "feat"),
        ),
        out_specs=(
            P(("groups", "rows"), "feat", None, None, None),
            P(("groups", "rows"), "feat", None),
        ),
        check_vma=False,
    )
```

```python
import functools
import math

import jax
import jax.numpy as jnp
import numpy as np
from jax import lax
from jax.experimental import pallas as pl
from jax.experimental.pallas import tpu as pltpu
from jax.sharding import PartitionSpec as P

SMEM = pl.BlockSpec(memory_space=pltpu.SMEM)
VMEM = pl.BlockSpec(memory_space=pltpu.VMEM)
HBM = pl.BlockSpec(memory_space=pltpu.HBM)
VMEM_LIMIT = 24 << 20


def parity_table(length):
    positions = np.arange(length)
    shared = positions[:, None] & positions[None, :]
    parity = np.zeros_like(shared)
    while shared.any():
        parity ^= shared & 1
        shared = shared >> 1
    return 1 - 2 * parity


def from_partner(block, axis, distance):
    count = lax.axis_size(axis)
    route = []
    for low in range(count):
        high = low | 1 << distance
        if high != low and high < count:
            route += [(low, high), (high, low)]
    return lax.ppermute(block, axis, route)


def passed_along(value, axis, steps):
    count = lax.axis_size(axis)
    pairs = [(source, (source + steps) % count) for source in range(count)]
    return lax.ppermute(value, axis, pairs)


def general(embeddings, signs, tile_blocks, tile_counts):
    groups = lax.axis_size("feat")
    feat_place = lax.axis_index("feat")
    row_place = lax.axis_index("rows")
    signed = embeddings * signs.astype(jnp.bfloat16)[:, None]
    regrouped = lax.all_to_all(signed, "feat", split_axis=1, concat_axis=0, tiled=True)
    features = regrouped.shape[0]
    block_rows = regrouped.shape[1]
    local_width = features // groups
    score_scale = 1.0 / math.sqrt(features)
    inner_table = jnp.asarray(parity_table(local_width), jnp.bfloat16)
    outer_table = jnp.asarray(parity_table(groups), jnp.float32)
    blocked = regrouped.reshape(groups, local_width, block_rows)
    first_section = jnp.einsum(
        "abr,bc->acr", blocked, inner_table, preferred_element_type=jnp.float32
    )
    turned = (
        jnp.einsum("acr,ad->dcr", first_section, outer_table, precision=lax.Precision.HIGHEST)
        * score_scale
    )
    flattened = turned.reshape(features, block_rows)
    norm_factor = lax.rsqrt(jnp.mean(flattened * flattened, axis=0, keepdims=True) + 1e-06)
    unit_rows = (flattened * norm_factor).astype(jnp.bfloat16).T
    following = passed_along(unit_rows, "feat", -1)
    partner = from_partner(unit_rows, "rows", 0)
    following_partner = from_partner(following, "rows", 0)
    candidates = jnp.stack([unit_rows, following, partner, following_partner])
    tile_total = tile_blocks.shape[2]
    own_list = lax.dynamic_index_in_dim(tile_blocks[:, 0, :], row_place, 0, keepdims=False)
    own_count = lax.dynamic_index_in_dim(tile_counts[:, 0], row_place, 0, keepdims=False)

    def add_tile(slot_index, buffer):
        block_id = own_list[slot_index]
        other_half = (block_id // groups != row_place).astype(jnp.int32)
        other_bucket = (block_id % groups != feat_place).astype(jnp.int32)
        keyed_block = lax.dynamic_index_in_dim(
            candidates, other_bucket + 2 * other_half, 0, keepdims=False
        )
        tile_value = (
            lax.dot_general(
                unit_rows, keyed_block, (((1,), (1,)), ((), ())), preferred_element_type=jnp.float32
            )
            * score_scale
        )
        return lax.dynamic_update_index_in_dim(buffer, tile_value, slot_index, 0)

    empty_tiles = jnp.zeros((tile_total, block_rows, block_rows), jnp.float32)
    result = lax.fori_loop(0, own_count, add_tile, empty_tiles)
    return (result[None, None], unit_rows[None])


ACROSS = 2
ALONG = 4


def signs_kernel(signs_ref, wide_ref):
    step = signs_ref.shape[1]
    for i in range(signs_ref.shape[0]):
        tile = jnp.broadcast_to(signs_ref[i : i + 1, :].astype(jnp.float32), (step, step))
        tile = tile.T.astype(jnp.bfloat16)
        for low in range(0, wide_ref.shape[1], step):
            wide_ref[i * step : (i + 1) * step, low : low + step] = tile


def wanted(hop):
    place = lax.axis_index("feat")
    side = lax.rem(place, ACROSS)
    first = ACROSS * lax.bitwise_xor(lax.div(place, ACROSS), hop)
    last = lax.rem(first + ACROSS, ACROSS * ALONG)
    return jnp.where(side == 0, first, last), first + 1, jnp.where(side == 0, last, first)


KEPT, MIDDLE, OTHER = range(3)
ROUTED_FIRST = (((0, MIDDLE), (0, OTHER)), ((1, MIDDLE), (1, OTHER)), ((2, MIDDLE), (2, OTHER)), ((3, OTHER),))
ROUTED_LATER = (((0, KEPT),), ((1, KEPT),), ((2, KEPT),), ((3, KEPT),), ((3, MIDDLE),))


def route_kernel(groups, emb_ref, *refs):
    first_call = groups is ROUTED_FIRST
    signs_ref, refs = refs[0], list(refs[1:])
    if first_call:
        sign_sem, sign_rows = refs.pop(), refs.pop()
        sign_copy = pltpu.make_async_copy(signs_ref, sign_rows, sign_sem)
        sign_copy.start()
    sems = refs.pop()
    wide_ref = refs.pop() if first_call else signs_ref
    targets = []
    for ref, blocks in zip(refs, groups):
        for i, (hop, kind) in enumerate(blocks):
            targets.append((ref.at[i] if len(blocks) > 1 else ref, wanted(hop)[kind]))
    copies = []
    for i, (ref, block) in enumerate(targets):
        rows = ref.shape[1]
        start = pl.multiple_of(block * rows, rows)
        copies.append(pltpu.make_async_copy(emb_ref.at[:, pl.ds(start, rows)], ref, sems.at[i]))
    for copy in copies:
        copy.start()
    if first_call:
        sign_copy.wait()
        signs_kernel(sign_rows, wide_ref)
    for copy, (ref, block) in zip(copies, targets):
        copy.wait()
        ref[...] = ref[...] * wide_ref[...]


def route(embeddings, signs, rows, groups):
    width = embeddings.shape[0]
    first_call = groups is ROUTED_FIRST
    shapes = [(width, rows) if len(blocks) == 1 else (len(blocks), width, rows) for blocks in groups]
    count = sum(len(blocks) for blocks in groups)
    scratch = [pltpu.SemaphoreType.DMA((count,))]
    if first_call:
        shapes.append((width, rows))
        signs = signs.reshape(width // 128, 128)
        scratch += [pltpu.VMEM(signs.shape, signs.dtype), pltpu.SemaphoreType.DMA]
        signs = pltpu.with_memory_space_constraint(signs, pltpu.HBM)
    return pl.pallas_call(
        functools.partial(route_kernel, groups),
        in_specs=[HBM, HBM if first_call else VMEM],
        out_specs=[VMEM] * len(shapes),
        out_shape=[jax.ShapeDtypeStruct(shape, jnp.bfloat16) for shape in shapes],
        scratch_shapes=scratch,
        compiler_params=pltpu.CompilerParams(vmem_limit_bytes=VMEM_LIMIT),
        cost_estimate=pl.CostEstimate(
            flops=count * width * rows, bytes_accessed=count * width * rows * 4, transcendentals=0
        ),
        name="route",
    )(pltpu.with_memory_space_constraint(embeddings, pltpu.HBM), signs)


def butterfly(parts):
    parts = list(parts)
    half = 1
    while half < len(parts):
        for low in range(0, len(parts), 2 * half):
            for i in range(low, low + half):
                a, b = parts[i], parts[i + half]
                parts[i], parts[i + half] = a + b, a - b
        half *= 2
    return parts


def turned_parts(pieces, table_ref, low, chunk):
    return butterfly(
        lax.dot_general(
            piece,
            table_ref[:, low : low + chunk],
            (((0,), (0,)), ((), ())),
            preferred_element_type=jnp.float32,
        )
        for piece in pieces
    )


def begin_kernel(picks, *refs):
    table_ref, out_ref = refs[-2:]
    place = lax.axis_index("feat")
    pieces = [pick(refs, place) for pick in picks]
    width = pieces[0].shape[0]
    chunk = 256
    for low in range(0, width, chunk):
        for i, part in enumerate(turned_parts(pieces, table_ref, low, chunk)):
            out_ref[:, i * width + low : i * width + low + chunk] = part


def begin(inputs, picks, table):
    count = len(picks)
    width, rows = inputs[0].shape[-2:]
    return pl.pallas_call(
        functools.partial(begin_kernel, picks),
        in_specs=[VMEM] * (len(inputs) + 1),
        out_specs=VMEM,
        out_shape=jax.ShapeDtypeStruct((rows, count * width), jnp.float32),
        compiler_params=pltpu.CompilerParams(vmem_limit_bytes=VMEM_LIMIT),
        cost_estimate=pl.CostEstimate(
            flops=2 * rows * count * width * width, bytes_accessed=3 << 20, transcendentals=0
        ),
        name="begin",
    )(*inputs, table)


def finish_kernel(picks, *refs):
    begun_ref, table_ref, out_ref, turned = refs[-4:]
    place = lax.axis_index("feat")
    pieces = [pick(refs, place) for pick in picks]
    width, rows = pieces[0].shape
    half = len(pieces)
    count = 2 * half
    features = count * width
    chunk = 256
    total = jnp.zeros((rows, 128), jnp.float32)
    for low in range(0, width, chunk):
        for i, late in enumerate(turned_parts(pieces, table_ref, low, chunk)):
            early = begun_ref[:, i * width + low : i * width + low + chunk]
            for place_out, part in ((i, early + late), (i + half, early - late)):
                turned[:, place_out * width + low : place_out * width + low + chunk] = part
                square = part * part
                for lane in range(0, chunk, 128):
                    total = total + square[:, lane : lane + 128]
    mean = jnp.sum(total, axis=1, keepdims=True) * (1.0 / (features * features))
    factor = lax.rsqrt(mean + 1e-06) * (1.0 / math.sqrt(features))
    for i in range(count):
        odd = jnp.int32(0)
        for bit in range(count.bit_length() - 1):
            if i >> bit & 1:
                odd = odd + (lax.shift_right_logical(place, bit) & 1)
        sign = (1 - 2 * (odd & 1)).astype(jnp.float32)
        columns = slice(i * width, (i + 1) * width)
        out_ref[:, columns] = (turned[:, columns] * (factor * sign)).astype(jnp.bfloat16)


def finish(inputs, picks, begun, table):
    count = 2 * len(picks)
    width, rows = inputs[0].shape[-2:]
    return pl.pallas_call(
        functools.partial(finish_kernel, picks),
        in_specs=[VMEM] * (len(inputs) + 2),
        out_specs=VMEM,
        out_shape=jax.ShapeDtypeStruct((rows, count * width), jnp.bfloat16),
        scratch_shapes=[pltpu.VMEM((rows, count * width), jnp.float32)],
        compiler_params=pltpu.CompilerParams(vmem_limit_bytes=VMEM_LIMIT),
        cost_estimate=pl.CostEstimate(
            flops=rows * count * width * width, bytes_accessed=5 << 20, transcendentals=0
        ),
        name="finish",
    )(*inputs, begun, table)


def listed(lists_ref, counts_ref, slot, groups):
    place = lax.axis_index("feat")
    half = lax.axis_index("rows")
    block_id = lists_ref[half, slot]
    other_half = (lax.div(block_id, groups) != half).astype(jnp.int32)
    own_bucket = (lax.rem(block_id, groups) == place).astype(jnp.int32)
    side = lax.rem(place, ACROSS)
    is_outer = (own_bucket != side).astype(jnp.int32)
    choice = is_outer + 2 * other_half
    return jnp.where(slot < counts_ref[half], choice, -1)


def product(query, key, features):
    return lax.dot_general(
        query, key, (((1,), (1,)), ((), ())), preferred_element_type=jnp.float32
    ) * (1.0 / math.sqrt(features))


def early_kernel(groups, lists_ref, counts_ref, mid_ref, outer_ref, mid2_ref, tiles_ref, unit_ref, out_sem):
    own_middle = lax.rem(lax.axis_index("feat"), ACROSS) == 1
    features = mid_ref.shape[1]
    keys = (mid_ref, outer_ref, mid2_ref)
    for value, query_ref in ((True, mid_ref), (False, outer_ref)):

        @pl.when(own_middle == value)
        def _(query_ref=query_ref):
            pltpu.make_async_copy(query_ref, unit_ref, out_sem).start()

    def fill(slot, carry):
        choice = listed(lists_ref, counts_ref, slot, groups)

        @pl.when((choice < 0) | (choice > 2))
        def _():
            tiles_ref[slot] = jnp.zeros(tiles_ref.shape[1:], jnp.float32)

        for value, query_ref in ((True, mid_ref), (False, outer_ref)):
            for index, key_ref in enumerate(keys):

                @pl.when((own_middle == value) & (choice == index))
                def _(query_ref=query_ref, key_ref=key_ref):
                    tiles_ref[slot] = product(query_ref[...], key_ref[...], features)

        return carry

    lax.fori_loop(0, tiles_ref.shape[0], fill, 0)
    pltpu.make_async_copy(mid_ref, unit_ref, out_sem).wait()


def late_kernel(groups, lists_ref, counts_ref, mid_ref, outer_ref, outer2_ref, early_ref, tiles_ref, tile, out_sem):
    own_middle = lax.rem(lax.axis_index("feat"), ACROSS) == 1
    features = mid_ref.shape[1]
    choices = [listed(lists_ref, counts_ref, slot, groups) for slot in range(early_ref.shape[0])]
    needed = functools.reduce(jnp.logical_or, [choice == 3 for choice in choices])
    slot = jnp.int32(0)
    for i, choice in enumerate(choices):
        slot = jnp.where(choice == 3, i, slot)
    for value, query_ref in ((True, mid_ref), (False, outer_ref)):

        @pl.when((own_middle == value) & needed)
        def _(query_ref=query_ref):
            tile[...] = product(query_ref[...], outer2_ref[...], features)

    @pl.when(needed)
    def _():
        out = pltpu.make_async_copy(tile, tiles_ref.at[slot], out_sem)
        out.start()
        out.wait()


def scores_early(lists, counts, mid, outer, mid2, groups):
    rows, features = mid.shape
    tiles = lists.shape[1]
    return pl.pallas_call(
        functools.partial(early_kernel, groups),
        in_specs=[SMEM, SMEM, VMEM, VMEM, VMEM],
        out_specs=[VMEM, HBM],
        out_shape=[
            jax.ShapeDtypeStruct((tiles, rows, rows), jnp.float32),
            jax.ShapeDtypeStruct((rows, features), jnp.bfloat16),
        ],
        scratch_shapes=[pltpu.SemaphoreType.DMA],
        compiler_params=pltpu.CompilerParams(vmem_limit_bytes=VMEM_LIMIT),
        cost_estimate=pl.CostEstimate(
            flops=4 * rows * rows * features, bytes_accessed=9 << 20, transcendentals=0
        ),
        name="early",
    )(lists, counts, mid, outer, mid2)


def scores_late(lists, counts, mid, outer, outer2, early, groups):
    rows, features = mid.shape
    return pl.pallas_call(
        functools.partial(late_kernel, groups),
        in_specs=[SMEM, SMEM, VMEM, VMEM, VMEM, HBM],
        out_specs=HBM,
        out_shape=jax.ShapeDtypeStruct(early.shape, early.dtype),
        scratch_shapes=[pltpu.VMEM((rows, rows), jnp.float32), pltpu.SemaphoreType.DMA],
        input_output_aliases={5: 0},
        compiler_params=pltpu.CompilerParams(vmem_limit_bytes=VMEM_LIMIT),
        cost_estimate=pl.CostEstimate(
            flops=2 * rows * rows * features, bytes_accessed=4 << 20, transcendentals=0
        ),
        name="late",
    )(lists, counts, mid, outer, outer2, early)


ORDER = (
    ("S2",),
    ("O3",),
    ("X0",),
    ("S1",),
    ("X1",),
    ("X2",),
    ("K1", "X0"),
    ("R2",),
    ("B3", "S2"),
    ("K3", "X1"),
    ("R3", "R2"),
    ("XO", "R2"),
    ("XB", "K1"),
    ("K2", "R3"),
)


ROUTE_AFTER = "S1"
MIDDLE_AFTER = ("K3", "R3")


def after(value, *events):
    return lax.optimization_barrier((value, *events))[0]


def chip(at, side):
    return ACROSS * at + side


EVERY = tuple(range(ACROSS * ALONG))
DIRECT = (chip(0, 0), chip(1, 1), chip(2, 0), chip(3, 1))
RELAYED = (chip(1, 0), chip(0, 1), chip(3, 0), chip(2, 1))
NEAR = 1
FAR = (2, 3)


def hop_over(value, axis, mask, receivers=None):
    if receivers is None:
        receivers = range(lax.axis_size(axis))
    return lax.ppermute(value, axis, [(to ^ mask, to) for to in receivers])


def along(value, hop, receivers=EVERY):
    return hop_over(value, "feat", ACROSS * hop, receivers)


def across(value):
    return hop_over(value, "feat", 1)


def plain(index, pick=None):
    if pick is None:
        return lambda refs, place: refs[index][...]
    return lambda refs, place: refs[index][pick]


def kept_far(direct, relayed):
    def read(refs, place):
        straight = lax.rem(lax.div(place, ACROSS) + lax.rem(place, ACROSS), 2) == 0
        return jnp.where(straight, refs[direct][...], refs[relayed][...])

    return read


def paired(embeddings, signs, tile_blocks, tile_counts):
    groups = lax.axis_size("feat")
    width, columns = embeddings.shape
    rows = columns // groups
    table = jnp.asarray(parity_table(width), jnp.bfloat16)
    S0, S1, S2, O3, wide = route(embeddings, signs, rows, ROUTED_FIRST)
    late = {}
    plan = {
        "S1": lambda got: (S1, along, 1),
        "S2": lambda got: (S2, along, 2),
        "B3": lambda got: (late["B3"], along, 3),
        "O3": lambda got: (O3, along, 3),
        "K1": lambda got: (late["K1"], along, 1),
        "K2": lambda got: (late["K2"], along, 2, DIRECT),
        "K3": lambda got: (late["K3"], along, 3, DIRECT),
        "X0": lambda got: (S0, across),
        "X1": lambda got: (got["S1"], across),
        "X2": lambda got: (got["S2"], across),
        "XB": lambda got: (got["B3"], across),
        "XO": lambda got: (got["O3"], across),
        "R2": lambda got: (got["S2"][1], along, NEAR, RELAYED),
        "R3": lambda got: (got["O3"], along, NEAR, RELAYED),
    }
    got = {}
    for name, *events in ORDER:
        if not late and ROUTE_AFTER in got:
            rest = route(embeddings, after(wide, got[ROUTE_AFTER]), rows, ROUTED_LATER)
            late = dict(zip(("K0", "K1", "K2", "K3", "B3"), rest))
        value, move, *rest = plan[name](got)
        if events:
            value = after(value, *(got.get(event, late.get(event)) for event in events))
        with jax.named_scope(name):
            got[name] = move(value, *rest)
    mid_begun = begin(
        [S0, got["X0"], got["S1"], got["X1"]], [plain(i, 0) for i in range(4)], table
    )
    outer_begun = begin(
        [late["K0"], got["X0"], got["K1"], got["X1"]],
        [plain(0), plain(1, 1), plain(2), plain(3, 1)],
        table,
    )
    first = after(got["S2"], *(got[name] for name in MIDDLE_AFTER))
    mid = finish(
        [first, got["X2"], got["B3"], got["XB"]],
        [plain(0, 0), plain(1, 0), plain(2), plain(3)],
        mid_begun,
        table,
    )
    mid2 = hop_over(mid, "rows", 1)
    outer = finish(
        [got["K2"], got["R3"], got["X2"], got["K3"], got["R2"], got["XO"]],
        [kept_far(0, 1), plain(2, 1), kept_far(3, 4), plain(5)],
        outer_begun,
        table,
    )
    outer2 = hop_over(outer, "rows", 1)
    lists = tile_blocks[:, 0, :]
    counts = tile_counts[:, 0]
    early, unit = scores_early(lists, counts, mid, outer, mid2, groups)
    tiles = scores_late(lists, counts, mid, outer, outer2, early, groups)
    return (tiles[None, None], unit[None])


def solution(mesh):
    body = paired if mesh.shape["feat"] == ALONG * ACROSS and mesh.shape["rows"] == 2 else general
    return jax.shard_map(
        body,
        mesh=mesh,
        in_specs=(
            P("feat", ("groups", "rows")),
            P("feat"),
            P("groups", "feat", None),
            P("groups", "feat"),
        ),
        out_specs=(
            P(("groups", "rows"), "feat", None, None, None),
            P(("groups", "rows"), "feat", None),
        ),
        check_vma=False,
    )
```
